128 devices in a mesh: rep: 8 (over y, z_lo), tp: 16 (over x, z_hi, core).
Axes of the slice: x: 4, y: 4, z: 4 (z_hi: 2, z_lo: 2; z = z_hi * 2 + z_lo), core: 2. Of those that a mesh axis runs over, the one named last changes fastest.
Arguments:
- embeds: bfloat16 [6272, 5120], P('rep', 'tp'), parts along dimension 0, may hold values from -6 to 6
- remask: int32 [6272], P('rep'), parts along dimension 0, may hold values 0 or 1
- lengths: int32 [32], P('rep'), parts along dimension 0, may hold values from 49 to 196, as said below
- mask_vec: bfloat16 [5120], P('tp'), may hold values from -6 to 6
- attn_gain: bfloat16 [5120], replicated, may hold values from 0.25 to 1.75
- w_query: bfloat16 [5120, 4096], P(None, 'tp'), may hold values from -0.078125 to 0.078125
- q_bias: bfloat16 [4096], P('tp'), may hold values from -200 to 200
- w_key: bfloat16 [5120, 1024], P(None, 'tp'), may hold values from -0.078125 to 0.078125
- w_value: bfloat16 [5120, 1024], P(None, 'tp'), may hold values from -0.078125 to 0.078125
- v_bias: bfloat16 [1024], P('tp'), may hold values from -3 to 3
- w_out: bfloat16 [4096, 5120], P('tp'), may hold values from -0.125 to 0.125
- head_gain: bfloat16 [5120], replicated, may hold values from 0.25 to 1.75
- w_head: bfloat16 [5120, 512], P(None, 'tp'), may hold values from -20 to 20
Outputs:
- hidden: bfloat16 [6272, 5120], P('rep', 'tp'), parts along dimension 0
- logprob: float32 [6272, 512], P('rep', 'tp'), parts along dimension 0
The draws below stay inside these ranges and needn't reach their ends.
There are 8 independent parts, one for each index of `rep`. The reference program is written for one: setup_inputs(seed, part) draws one part's arguments, and reference() takes and returns one part's arrays. A program takes and returns all parts, laid end to end along the dimension named above; an argument that names none is the same for every part. Nothing has to cross between parts.
Inputs may be any that keep to these rules, and one draw needn't show every extreme that they name: `lengths`: every request has at least 49 tokens, and one request of each part has exactly 196.
All inputs are finite; a program needn't handle non-finite values.
Results may differ from the reference program's by a relative error of at most 0.018.
The reference program's roundings to bfloat16 on the way (of `masked`, `normed`, `attn_prob`, `context` and `normed_head`) count: a program that leaves them out, or rounds other values in their place, can miss the bound.
Values may be sent and summed in bfloat16 or wider, within the bound.
A program may use at most 128 MiB of HBM per device.

```python
import jax
import jax.numpy as jnp
from jax import lax

D = 5120
HEADS = 32
KVH = 8
HS = 128
VOCAB = 512
L = 196
REQS = 4
TOKENS = 784


def draw_lengths(key, part):
    first_key = jax.random.fold_in(key, 11)
    second_key = jax.random.fold_in(key, 12)
    drawn = jax.random.randint(first_key, (REQS,), L // 4, L + 1)
    chosen = jax.random.randint(second_key, (), 0, REQS)
    return jnp.where(jnp.arange(REQS) == chosen, L, drawn).astype(jnp.int32)


def draw_q_bias(key, part):
    base = jnp.clip(jax.random.normal(jax.random.fold_in(key, 21), (HEADS * HS,), jnp.float32), -4.0, 4.0)
    return (0.5 * base).astype(jnp.bfloat16)


def draw_w_head(key, part):
    base = jnp.clip(jax.random.normal(jax.random.fold_in(key, 31), (D, VOCAB), jnp.float32), -4.0, 4.0)
    return (base * (3.0 / D ** 0.5)).astype(jnp.bfloat16)


def touch_ends(entries, own_key, smallest, largest):
    extent = entries.shape
    spot = [jax.random.randint(jax.random.fold_in(own_key, axis), (), 0, extent[axis]) for axis in range(len(extent))]
    entries = entries.at[tuple(spot)].set(smallest)
    longest = extent.index(max(extent))
    spot[longest] = (spot[longest] + 1) % extent[longest]
    return entries.at[tuple(spot)].set(largest)


def with_spikes(values, stream_key, source, target, blocks, factor):
    def block_of(dim):
        return (jnp.arange(values.shape[dim]) // (values.shape[dim] // blocks)).reshape((-1,) + (1,) * (values.ndim - 1 - dim))

    one_side = jax.random.permutation(stream_key, blocks)[block_of(target)]
    other_side = (block_of(target) + blocks // 2) % blocks
    return jnp.where((block_of(source) == one_side) | (block_of(source) == other_side), factor * values, values)


def shard_levels(rng, extent, pieces, low, high):
    def one(axis_at, parts):
        draws = jax.random.uniform(jax.random.fold_in(jax.random.fold_in(rng, 6), axis_at), (parts,), jnp.float32, low / len(pieces), high / len(pieces))
        return jnp.repeat(jnp.exp(draws), extent[axis_at] // parts).reshape((-1,) + (1,) * (len(extent) - axis_at - 1))

    factor_of = one(*pieces[0])
    for cut in pieces[1:]:
        factor_of = factor_of * one(*cut)
    return factor_of


def normal_values(rng, extent, scale, most, pieces=(), kind=jnp.bfloat16):
    values = scale * jax.random.normal(rng, extent, jnp.float32)
    if pieces:
        values = values * shard_levels(rng, extent, pieces, -0.22, 0.18)
    return jnp.clip(values, -most, most).astype(kind)


def bell_draw_with(own_key, extent, spread, limit, pieces, heavy, kind=jnp.bfloat16):
    values = spread * jax.random.normal(own_key, extent, jnp.float32)
    if pieces:
        values = values * shard_levels(own_key, extent, pieces, -0.22, 0.18)
    return jnp.clip(with_spikes(values, jax.random.fold_in(own_key, 3), *heavy), -limit, limit).astype(kind)


def setup_inputs(seed: int = 0, part: int = 0) -> dict:
    seeds = jax.random.split(jax.random.key(seed), 14)
    own_keys = jax.random.split(jax.random.fold_in(seeds[13], part), 14)
    embeds = normal_values(own_keys[0], (TOKENS, D), 1.0, 6.0, ((1, 16),))
    remask = touch_ends((jax.random.randint(own_keys[1], (TOKENS,), 0, 2) < 1).astype(jnp.int32), jax.random.fold_in(own_keys[1], 1), 0, 1)
    lengths = draw_lengths(jax.random.fold_in(jax.random.fold_in(seeds[13], part), 71), part)
    mask_vec = normal_values(seeds[3], (D,), 1.0, 6.0, ((0, 16),))
    attn_gain = jnp.clip(1.0 + 0.15 * jax.random.normal(seeds[4], (D,), jnp.float32), 0.25, 1.75).astype(jnp.bfloat16)
    w_query = normal_values(seeds[5], (D, HEADS * HS), D ** -0.5, 0.078125, ((1, 16),))
    q_bias = draw_q_bias(jax.random.fold_in(seeds[13], 71), part)
    w_key = normal_values(seeds[7], (D, KVH * HS), D ** -0.5, 0.078125, ((1, 16),))
    w_value = normal_values(seeds[8], (D, KVH * HS), D ** -0.5, 0.078125, ((1, 16),))
    v_bias = normal_values(seeds[9], (KVH * HS,), 0.5, 3.0, ((0, 16),))
    w_out = bell_draw_with(seeds[10], (HEADS * HS, D), (HEADS * HS) ** -0.5, 0.125, ((0, 16),), (0, 1, 16, 2.0))
    head_gain = jnp.clip(1.0 + 0.15 * jax.random.normal(seeds[11], (D,), jnp.float32), 0.25, 1.75).astype(jnp.bfloat16)
    w_head = draw_w_head(jax.random.fold_in(seeds[13], 71), part)
    return {"embeds": embeds, "remask": remask, "lengths": lengths, "mask_vec": mask_vec, "attn_gain": attn_gain, "w_query": w_query, "q_bias": q_bias, "w_key": w_key, "w_value": w_value, "v_bias": v_bias, "w_out": w_out, "head_gain": head_gain, "w_head": w_head}


EPS = 1e-06

def rms_norm(matrix, gain):
    wide = matrix.astype(jnp.float32)
    inverse = lax.rsqrt(lax.optimization_barrier(jnp.mean(wide * wide, axis=-1, keepdims=True)) + EPS)
    return (wide * inverse * gain.astype(jnp.float32)).astype(jnp.bfloat16)

def reference(embeds, remask, lengths, mask_vec, attn_gain, w_query, q_bias, w_key, w_value, v_bias, w_out, head_gain, w_head):
    masked = jnp.where(remask[:, None] == 1, mask_vec[None, :], embeds)
    normed = rms_norm(masked, attn_gain)
    queries = (jnp.dot(normed, w_query, preferred_element_type=jnp.float32) + q_bias.astype(jnp.float32)).astype(jnp.bfloat16)
    key_rows = jnp.dot(normed, w_key, preferred_element_type=jnp.float32).astype(jnp.bfloat16)
    value_rows = (jnp.dot(normed, w_value, preferred_element_type=jnp.float32) + v_bias.astype(jnp.float32)).astype(jnp.bfloat16)
    group = HEADS // KVH
    q_four = queries.reshape(REQS, L, HEADS, HS).astype(jnp.float32)
    k_four = jnp.repeat(key_rows.reshape(REQS, L, KVH, HS), group, axis=2).astype(jnp.float32)
    v_four = jnp.repeat(value_rows.reshape(REQS, L, KVH, HS), group, axis=2).astype(jnp.float32)
    scores = jnp.einsum('rqhd,rkhd->rhqk', q_four, k_four) * HS ** (-0.5)
    valid = jnp.arange(L, dtype=jnp.int32)[None, :] < lengths[:, None]
    scores = jnp.where(valid[:, None, None, :], scores, jnp.float32(-1e+30))
    peak = lax.optimization_barrier(jnp.max(scores, axis=-1, keepdims=True))
    expo = jnp.exp(scores - peak)
    attn_prob = (expo / lax.optimization_barrier(jnp.sum(expo, axis=-1, keepdims=True))).astype(jnp.bfloat16)
    context = jnp.einsum('rhqk,rkhd->rqhd', attn_prob.astype(jnp.float32), v_four).astype(jnp.bfloat16)
    context = context.reshape(TOKENS, HEADS * HS)
    summed = jnp.dot(context, w_out, preferred_element_type=jnp.float32)
    hidden = (masked.astype(jnp.float32) + summed).astype(jnp.bfloat16)
    normed_head = rms_norm(hidden, head_gain)
    logits = jnp.dot(normed_head, w_head, preferred_element_type=jnp.float32)
    top = lax.optimization_barrier(jnp.max(logits, axis=-1, keepdims=True))
    log_total = top + jnp.log(lax.optimization_barrier(jnp.sum(jnp.exp(logits - top), axis=-1, keepdims=True)))
    return (hidden, logits - log_total)
```

```python
import jax
import jax.numpy as jnp
from jax import lax
from jax.experimental import pallas as pl
from jax.experimental.pallas import tpu as pltpu
from jax.sharding import PartitionSpec as P

HS = 128
L = 196
ROWS = 200
LANES = 256
CHIPS = 8
WIDE = 640
D = 5120
HALF = 320
EPS = 1e-06
MESH = pl.DeviceIdType.MESH
F32 = jnp.float32
BF16 = jnp.bfloat16

SIB_X, SIB_WQ, SIB_WK, SIB_WV, SIB_WO, SIB_SMALL, SIB_HEAD = 0, 2, 3, 4, 5, 6, 7
AG = 8
RS = AG + 14
HEAD = RS + 14
LOGIT = HEAD + 7
STAT = LOGIT + 14
SIB_HID = STAT + 14
SIB_LP = SIB_HID + 2
COPIES = SIB_LP + 2


def dot_nt(a, b):
    return lax.dot_general(a, b, (((1,), (1,)), ((), ())), preferred_element_type=F32)


def kernel(
    lengths,
    x4,
    small,
    gains,
    wq_in,
    wk_in,
    wv_in,
    wo_in,
    wh_in,
    hid_out,
    lp_out,
    sib_x,
    xg,
    wq,
    wkv,
    wo,
    whp,
    whg,
    sm,
    acc_q,
    acc_kv,
    q_ref,
    k_ref,
    v_ref,
    ctx,
    stage,
    got,
    hid,
    hid_send,
    lmsg,
    lgot,
    smsg,
    sgot,
    lp_send,
    ssem,
    rsem,
    lsem,
):
    me = lax.axis_index("tp")
    x = me // 4
    zh = lax.rem(me // 2, 2)
    c = lax.rem(me, 2)
    chip = me // 2
    zo = 1 - zh
    xp, xm, xx = lax.rem(x + 1, 4), lax.rem(x + 3, 4), lax.rem(x + 2, 4)

    def core(xs, zs):
        return {"tp": xs * 4 + zs * 2 + c}

    def block(xs, zs):
        return xs * 2 + zs

    sibling = {"tp": me + 1 - 2 * c}
    others = [lax.rem(chip + d, CHIPS) for d in range(1, CHIPS)]
    started = []

    def send(number, src, dst, target):
        copy = pltpu.make_async_remote_copy(
            src_ref=src,
            dst_ref=dst,
            send_sem=ssem.at[number],
            recv_sem=rsem.at[number],
            device_id=target,
            device_id_type=MESH,
        )
        copy.start()
        started.append(copy)
        return copy

    barrier = pltpu.get_barrier_semaphore()
    pl.semaphore_signal(barrier, inc=1, device_id=sibling, device_id_type=MESH)
    for other in others:
        pl.semaphore_signal(
            barrier, inc=1, device_id={"tp": other * 2 + c}, device_id_type=MESH
        )
    krows = pl.ds(pl.multiple_of(c * 64, 64), 64)
    vrows = pl.ds(pl.multiple_of(128 + c * 64, 64), 64)
    orows = pl.ds(pl.multiple_of(c * 256, 256), 256)
    local = [
        pltpu.make_async_copy(wq_in, wq.at[c], lsem.at[0]),
        pltpu.make_async_copy(wk_in, wkv.at[krows], lsem.at[1]),
        pltpu.make_async_copy(wv_in, wkv.at[vrows], lsem.at[2]),
        pltpu.make_async_copy(wo_in, wo.at[orows], lsem.at[3]),
        pltpu.make_async_copy(small, sm.at[c], lsem.at[4]),
        pltpu.make_async_copy(
            wh_in.at[:, pl.ds(pl.multiple_of(chip * WIDE, WIDE), WIDE)],
            whp.at[c, chip],
            lsem.at[5],
        ),
    ]
    for copy in local:
        copy.start()
    k_ref[ROWS:, :] = jnp.zeros((LANES - ROWS, HS), BF16)
    v_ref[ROWS:, :] = jnp.zeros((LANES - ROWS, HS), BF16)
    hid[ROWS:, :] = jnp.zeros((LANES - ROWS, WIDE), BF16)
    pl.semaphore_wait(barrier, 8)

    sib = [
        send(SIB_X + r, x4.at[2 * (1 - c) + r], sib_x.at[r], sibling) for r in range(2)
    ]
    sib_w = [
        send(SIB_SMALL, small, sm.at[c], sibling),
        send(SIB_WQ, wq_in, wq.at[c], sibling),
        send(SIB_WK, wk_in, wkv.at[krows], sibling),
        send(SIB_WV, wv_in, wkv.at[vrows], sibling),
        send(SIB_WO, wo_in, wo.at[orows], sibling),
    ]

    ag = [[None] * 7 for _ in range(2)]
    rs = [[None] * 7 for _ in range(2)]
    near = {1: xp, -1: xm}
    way = (1, -1)

    for r in range(2):
        sib[r].wait_recv()
        mine, theirs = x4[2 * c + r], sib_x[r]
        left = jnp.where(c == 0, mine, theirs)
        right = jnp.where(c == 0, theirs, mine)
        xg[r, chip] = jnp.concatenate([left, right], axis=1)
        here = xg.at[r, chip]
        ag[r][0] = send(AG + 7 * r, here, here, core(xp, zh))
        ag[r][1] = send(AG + 7 * r + 1, here, here, core(xm, zh))
        ag[r][2] = send(AG + 7 * r + 2, here, here, core(x, zo))

    for r in range(2):
        w = way[r]
        base = AG + 7 * r
        ag[r][0].wait_recv()
        ag[r][1].wait_recv()
        part = xg.at[r, block(near[-w], zh)]
        ag[r][3] = send(base + 3, part, part, core(near[w], zh))
        ag[r][2].wait_recv()
        part = xg.at[r, block(x, zo)]
        ag[r][4] = send(base + 4, part, part, core(xp, zh))
        ag[r][5] = send(base + 5, part, part, core(xm, zh))
    head = [
        send(
            HEAD + d,
            wh_in.at[:, pl.ds(pl.multiple_of(other * WIDE, WIDE), WIDE)],
            whp.at[c, chip],
            {"tp": other * 2 + c},
        )
        for d, other in enumerate(others)
    ]
    for r in range(2):
        ag[r][3].wait_recv()
        part = xg.at[r, block(xx, zh)]
        ag[r][6] = send(AG + 7 * r + 6, part, part, core(x, zo))

    for copy in local:
        copy.wait()
    for copy in sib_w:
        copy.wait_recv()
    q_bias = [sm[p, 0:1, :] for p in range(2)]
    v_bias = sm[0, 1:2, 0:HS] + sm[1, 2:3, 0:HS]

    def project(xs, zs):
        columns = pl.ds(pl.multiple_of(block(xs, zs) * WIDE, WIDE), WIDE)
        return jnp.dot(ctx[...], wo[:, columns], preferred_element_type=F32)

    def attend(r):
        ag[r][4].wait_recv()
        ag[r][5].wait_recv()
        ag[r][6].wait_recv()

        def square(j, total):
            wide = xg[r, j].astype(F32)
            return total + jnp.sum(wide * wide, axis=1, keepdims=True)

        total = lax.fori_loop(0, CHIPS, square, jnp.zeros((ROWS, 1), F32))
        inverse = lax.rsqrt(total * (1.0 / D) + EPS)
        acc_q[...] = jnp.zeros_like(acc_q)
        acc_kv[...] = jnp.zeros_like(acc_kv)

        def lap(j, carry):
            gain = gains[0, pl.ds(j, 1), :]
            normed = (xg[r, j].astype(F32) * inverse * gain).astype(BF16)
            depth = pl.ds(pl.multiple_of(j * WIDE, WIDE), WIDE)
            for p in range(2):
                acc_q[p] += jnp.dot(normed, wq[p, depth, :], preferred_element_type=F32)
            acc_kv[...] += dot_nt(normed, wkv[:, depth])
            return carry

        lax.fori_loop(0, CHIPS, lap, 0)
        for p in range(2):
            q_ref[p] = (acc_q[p] + q_bias[p]).astype(BF16)
        k_ref[0:ROWS, :] = acc_kv[:, 0:HS].astype(BF16)
        v_ref[0:ROWS, :] = (acc_kv[:, HS:] + v_bias).astype(BF16)
        length = lengths[2 * c + r]
        valid = lax.broadcasted_iota(jnp.int32, (ROWS, LANES), 1) < length
        for n in range(4):
            at = slice((n % 2) * HS, (n % 2 + 1) * HS)
            scores = dot_nt(q_ref[n // 2, :, at], k_ref[...]) * HS ** (-0.5)
            scores = jnp.where(valid, scores, F32(-1e30))
            peak = jnp.max(scores, axis=1, keepdims=True)
            expo = jnp.exp(scores - peak)
            prob = (expo / jnp.sum(expo, axis=1, keepdims=True)).astype(BF16)
            ctx[:, n * HS : (n + 1) * HS] = jnp.dot(
                prob, v_ref[...], preferred_element_type=F32
            ).astype(BF16)

    def put(r, slot, value, target):
        stage[r, slot] = value.astype(BF16)
        rs[r][slot] = send(RS + 7 * r + slot, stage.at[r, slot], got.at[r, slot], target)

    def take(r, slot):
        rs[r][slot].wait_recv()
        return got[r, slot].astype(F32)

    for r in range(2):
        w = way[r]
        attend(r)
        put(r, 0, project(xx, zo), core(x, zo))
        put(r, 1, project(xp, zo), core(xp, zh))
        put(r, 2, project(xm, zo), core(xm, zh))
        put(r, 3, project(near[-w], zh), core(near[-w], zh))
        stage[r, 4] = project(xx, zh).astype(BF16)
        stage[r, 5] = project(x, zo).astype(BF16)
        stage[r, 6] = project(near[w], zh).astype(BF16)
        own = (project(x, zh)).astype(BF16)
        stage[r, 7] = own

    def staged(r, slot):
        return stage[r, slot].astype(F32)

    for r in range(2):
        put(r, 4, staged(r, 4) + take(r, 0), core(near[way[r]], zh))
        put(r, 5, staged(r, 5) + take(r, 1) + take(r, 2), core(x, zo))
    for r in range(2):
        put(r, 6, staged(r, 6) + take(r, 4), core(near[way[r]], zh))

    for copy in head:
        copy.wait_recv()
    sib_head = send(SIB_HEAD, whp.at[c], whp.at[c], sibling)
    sib_head.wait_recv()
    head_gain = gains[1, pl.ds(chip, 1), :]
    for p in range(2):
        raw = whp[p].reshape(CHIPS * 32, WIDE).astype(F32)
        whg[p] = (raw * head_gain).astype(BF16)

    sib_hid = []
    logit = [[], []]
    for r in range(2):
        summed = staged(r, 7) + take(r, 3) + take(r, 6) + take(r, 5)
        hidden = (xg[r, chip].astype(F32) + summed).astype(BF16)
        hid[0:ROWS, :] = hidden
        left, right = hidden[:, 0:HALF], hidden[:, HALF:]
        hid_out[2 * c + r] = jnp.where(c == 0, left, right)
        hid_send[r] = jnp.where(c == 0, right, left)
        sib_hid.append(
            send(SIB_HID + r, hid_send.at[r], hid_out.at[2 * c + r], sibling)
        )
        wide = hid[...].astype(F32)
        squares = jnp.sum(wide * wide, axis=1, keepdims=True)
        squares = jnp.broadcast_to(squares, (LANES, HS)).T[0:16]
        high = squares.astype(BF16).astype(F32)
        rest = squares - high
        mid = rest.astype(BF16).astype(F32)
        low = rest - mid
        row = lax.broadcasted_iota(jnp.int32, (16, LANES), 0)
        packed = jnp.where(
            row == 0, high, jnp.where(row == 1, mid, jnp.where(row == 2, low, 0.0))
        ).astype(BF16)
        for p in range(2):
            part = dot_nt(whg[p], hid[...]).astype(BF16)
            for i in range(CHIPS):
                lmsg[r, i, p * 32 : (p + 1) * 32, :] = part[i * 32 : (i + 1) * 32]
        for i in range(CHIPS):
            lmsg[r, i, 64:80, :] = packed
        for d, other in enumerate(others):
            logit[r].append(
                send(
                    LOGIT + 7 * r + d,
                    lmsg.at[r, other],
                    lgot.at[r, chip],
                    {"tp": other * 2 + c},
                )
            )
        lgot[r, chip] = lmsg[r, chip]

    logits = [None, None]
    stats = [[], []]
    for r in range(2):
        for copy in logit[r]:
            copy.wait_recv()
        total = lgot[r, 0].astype(F32)
        for i in range(1, CHIPS):
            total = total + lgot[r, i].astype(F32)
        squares = total[64:65] + total[65:66] + total[66:67]
        inverse = lax.rsqrt(squares * (1.0 / D) + EPS)
        logits[r] = total[0:64] * inverse
        top = jnp.max(logits[r], axis=0, keepdims=True)
        mass = jnp.sum(jnp.exp(logits[r] - top), axis=0, keepdims=True)
        row = lax.broadcasted_iota(jnp.int32, (8, LANES), 0)
        smsg[r] = jnp.where(row == 0, top, mass)
        for d, other in enumerate(others):
            stats[r].append(
                send(STAT + 7 * r + d, smsg.at[r], sgot.at[r, chip], {"tp": other * 2 + c})
            )
        sgot[r, chip] = smsg[r]

    sib_lp = []
    for r in range(2):
        for copy in stats[r]:
            copy.wait_recv()
        top = sgot[r, 0, 0:1, :]
        for i in range(1, CHIPS):
            top = jnp.maximum(top, sgot[r, i, 0:1, :])
        mass = jnp.zeros((1, LANES), F32)
        for i in range(CHIPS):
            mass = mass + sgot[r, i, 1:2, :] * jnp.exp(sgot[r, i, 0:1, :] - top)
        logprob = logits[r] - (top + jnp.log(mass))
        first, second = logprob[0:32], logprob[32:64]
        lp_out[2 * c + r] = jnp.where(c == 0, first, second)
        lp_send[r] = jnp.where(c == 0, second, first)
        sib_lp.append(send(SIB_LP + r, lp_send.at[r], lp_out.at[2 * c + r], sibling))
    for copy in sib_hid + sib_lp:
        copy.wait_recv()
    for copy in started:
        copy.wait_send()


def on_device(
    embeds,
    remask,
    lengths,
    mask_vec,
    attn_gain,
    w_query,
    q_bias,
    w_key,
    w_value,
    v_bias,
    w_out,
    head_gain,
    w_head,
):
    masked = jnp.where(remask[:, None] == 1, mask_vec[None, :], embeds)
    x4 = jnp.pad(masked.reshape(4, L, HALF), ((0, 0), (0, ROWS - L), (0, 0)))
    vb = v_bias.astype(F32)
    small = jnp.stack(
        [
            q_bias.astype(F32),
            jnp.pad(vb, (0, 192)),
            jnp.pad(vb, (64, 128)),
        ]
    )
    small = jnp.pad(small, ((0, 5), (0, 0)))
    gains = jnp.stack([attn_gain, head_gain]).astype(F32).reshape(2, CHIPS, WIDE)
    vmem = pl.BlockSpec(memory_space=pltpu.VMEM)
    anywhere = pl.BlockSpec(memory_space=pl.ANY)
    hid_out, lp_out = pl.pallas_call(
        kernel,
        out_shape=(
            jax.ShapeDtypeStruct((4, ROWS, HALF), BF16),
            jax.ShapeDtypeStruct((4, 32, LANES), F32),
        ),
        in_specs=[pl.BlockSpec(memory_space=pltpu.SMEM), vmem, vmem, vmem] + [anywhere] * 5,
        out_specs=(vmem, vmem),
        scratch_shapes=[
            pltpu.VMEM((2, ROWS, HALF), BF16),
            pltpu.VMEM((2, CHIPS, ROWS, WIDE), BF16),
            pltpu.VMEM((2, D, 256), BF16),
            pltpu.VMEM((256, D), BF16),
            pltpu.VMEM((512, D), BF16),
            pltpu.VMEM((2, CHIPS, 32, WIDE), BF16),
            pltpu.VMEM((2, CHIPS * 32, WIDE), BF16),
            pltpu.VMEM((2, 8, 256), F32),
            pltpu.VMEM((2, ROWS, 256), F32),
            pltpu.VMEM((ROWS, 256), F32),
            pltpu.VMEM((2, ROWS, 256), BF16),
            pltpu.VMEM((LANES, HS), BF16),
            pltpu.VMEM((LANES, HS), BF16),
            pltpu.VMEM((ROWS, 512), BF16),
            pltpu.VMEM((2, 8, ROWS, WIDE), BF16),
            pltpu.VMEM((2, 7, ROWS, WIDE), BF16),
            pltpu.VMEM((LANES, WIDE), BF16),
            pltpu.VMEM((2, ROWS, HALF), BF16),
            pltpu.VMEM((2, CHIPS, 80, LANES), BF16),
            pltpu.VMEM((2, CHIPS, 80, LANES), BF16),
            pltpu.VMEM((2, 8, LANES), F32),
            pltpu.VMEM((2, CHIPS, 8, LANES), F32),
            pltpu.VMEM((2, 32, LANES), F32),
            pltpu.SemaphoreType.DMA((COPIES,)),
            pltpu.SemaphoreType.DMA((COPIES,)),
            pltpu.SemaphoreType.DMA((6,)),
        ],
        compiler_params=pltpu.CompilerParams(
            collective_id=0, has_side_effects=True, vmem_limit_bytes=56 << 20
        ),
        name="refine",
    )(
        lengths,
        x4,
        small,
        gains,
        w_query,
        w_key.T,
        w_value.T,
        w_out,
        w_head.T,
    )
    hidden = hid_out[:, :L].reshape(4 * L, HALF)
    logprob = lp_out[:, :, :L].transpose(0, 2, 1).reshape(4 * L, 32)
    return hidden, logprob


def solution(mesh):
    placed = (
        P("rep", "tp"),
        P("rep"),
        P("rep"),
        P("tp"),
        P(),
        P(None, "tp"),
        P("tp"),
        P(None, "tp"),
        P(None, "tp"),
        P("tp"),
        P("tp", None),
        P(),
        P(None, "tp"),
    )
    return jax.shard_map(
        on_device,
        mesh=mesh,
        in_specs=placed,
        out_specs=(P("rep", "tp"), P("rep", "tp")),
        check_vma=False,
    )
```

```python
import jax
import jax.numpy as jnp
from jax import lax
from jax.experimental import pallas as pl
from jax.experimental.pallas import tpu as pltpu
from jax.sharding import PartitionSpec as P

HS = 128
L = 196
ROWS = 200
LANES = 256
CHIPS = 8
WIDE = 640
D = 5120
HALF = 320
TOKENS = 784
EPS = 1e-06
MESH = pl.DeviceIdType.MESH
F32 = jnp.float32
BF16 = jnp.bfloat16

SIB_X, SIB_WQ, SIB_WK, SIB_WV, SIB_WO, SIB_HEAD, SIB_QB, SIB_VB = 0, 2, 3, 4, 5, 6, 7, 8
AG = 9
RS = AG + 14
HEAD = RS + 14
LOGIT = HEAD + 7
STAT = LOGIT + 14
SIB_HID = STAT + 7
SIB_LP = SIB_HID + 2
COPIES = SIB_LP + 1


def dot_nt(a, b):
    return lax.dot_general(a, b, (((1,), (1,)), ((), ())), preferred_element_type=F32)


def lane_sums(wide):
    squares = wide * wide
    parts = squares[:, 0:128]
    for k in range(1, 5):
        parts = parts + squares[:, k * 128 : (k + 1) * 128]
    return jnp.sum(parts.T, axis=0, keepdims=True)


def kernel(
    lengths,
    embeds_in,
    remask_in,
    mask_vec_in,
    attn_gain_in,
    head_gain_in,
    qb_in,
    vb_in,
    wq_in,
    wk_in,
    wv_in,
    wo_in,
    wh_in,
    hid_out,
    lp_out,
    embeds,
    remask,
    mask_vec,
    attn_gain,
    head_gain,
    qb_mine,
    qb_theirs,
    vb_mine,
    vb_theirs,
    gains,
    masked,
    mine,
    sib_send,
    sib_x,
    xg,
    wq,
    wkv,
    wo,
    whp,
    whg,
    xn,
    ss,
    q_ref,
    k_ref,
    v_ref,
    ctx,
    kept,
    stage,
    got,
    hid,
    hid_send,
    hid_got,
    hid_mine,
    hid_all,
    lmsg,
    lgot,
    smsg,
    sgot,
    lp_send,
    lp_all,
    ssem,
    rsem,
    lsem,
):
    me = lax.axis_index("tp")
    x = me // 4
    zh = lax.rem(me // 2, 2)
    c = lax.rem(me, 2)
    chip = me // 2
    zo = 1 - zh
    xp, xm, xx = lax.rem(x + 1, 4), lax.rem(x + 3, 4), lax.rem(x + 2, 4)

    def core(xs, zs):
        return {"tp": xs * 4 + zs * 2 + c}

    def block(xs, zs):
        return xs * 2 + zs

    sibling = {"tp": me + 1 - 2 * c}
    others = [lax.rem(chip + d, CHIPS) for d in range(1, CHIPS)]
    started = []

    def send(number, src, dst, target):
        copy = pltpu.make_async_remote_copy(
            src_ref=src,
            dst_ref=dst,
            send_sem=ssem.at[number],
            recv_sem=rsem.at[number],
            device_id=target,
            device_id_type=MESH,
        )
        copy.start()
        started.append(copy)
        return copy

    barrier = pltpu.get_barrier_semaphore()
    for near_device in (sibling, core(xp, zh), core(xm, zh), core(x, zo)):
        pl.semaphore_signal(barrier, inc=1, device_id=near_device, device_id_type=MESH)
    krows = pl.ds(pl.multiple_of(c * 64, 64), 64)
    vrows = pl.ds(pl.multiple_of(128 + c * 64, 64), 64)
    orows = pl.ds(pl.multiple_of(c * 256, 256), 256)
    early = [
        pltpu.make_async_copy(embeds_in, embeds, lsem.at[0]),
        pltpu.make_async_copy(remask_in, remask, lsem.at[1]),
        pltpu.make_async_copy(mask_vec_in, mask_vec, lsem.at[2]),
    ]
    local = [
        pltpu.make_async_copy(attn_gain_in, attn_gain, lsem.at[3]),
        pltpu.make_async_copy(head_gain_in, head_gain, lsem.at[4]),
        pltpu.make_async_copy(qb_in, qb_mine, lsem.at[5]),
        pltpu.make_async_copy(vb_in, vb_mine, lsem.at[6]),
        pltpu.make_async_copy(wq_in, wq.at[c], lsem.at[7]),
        pltpu.make_async_copy(wk_in, wkv.at[krows], lsem.at[8]),
        pltpu.make_async_copy(wv_in, wkv.at[vrows], lsem.at[9]),
    ]
    later = [
        pltpu.make_async_copy(wo_in, wo.at[orows], lsem.at[10]),
        pltpu.make_async_copy(
            wh_in.at[:, pl.ds(pl.multiple_of(chip * WIDE, WIDE), WIDE)],
            whp.at[c, chip],
            lsem.at[11],
        ),
    ]
    for copy in early + local + later:
        copy.start()
    k_ref[ROWS:, :] = jnp.zeros((LANES - ROWS, HS), BF16)
    v_ref[ROWS:, :] = jnp.zeros((LANES - ROWS, HS), BF16)
    hid[ROWS:, :] = jnp.zeros((LANES - ROWS, WIDE), BF16)
    for copy in early:
        copy.wait()
    flags = remask[...][None, :]
    fill = jnp.broadcast_to(mask_vec[...].astype(F32)[None, :], (8, HALF)).T[:, 0:1]
    masked[TOKENS:, :] = jnp.zeros((8, HALF), F32)
    for k in range(7):
        at = slice(128 * k, min(128 * (k + 1), TOKENS))
        masked[at, :] = jnp.where(flags[:, at] == 1, fill, embeds[:, at].astype(F32)).T
    for r in range(2):
        low, high = masked[L * r : L * r + ROWS], masked[L * (r + 2) : L * (r + 2) + ROWS]
        mine[r] = jnp.where(c == 0, low, high)
        sib_send[r] = jnp.where(c == 0, high, low).astype(BF16)
    pl.semaphore_wait(barrier, 4)

    sib = [send(SIB_X + r, sib_send.at[r], sib_x.at[r], sibling) for r in range(2)]
    sib_w = [
        send(SIB_QB, qb_in, qb_theirs, sibling),
        send(SIB_VB, vb_in, vb_theirs, sibling),
        send(SIB_WQ, wq_in, wq.at[c], sibling),
        send(SIB_WK, wk_in, wkv.at[krows], sibling),
        send(SIB_WV, wv_in, wkv.at[vrows], sibling),
        send(SIB_WO, wo_in, wo.at[orows], sibling),
    ]

    ag = [[None] * 7 for _ in range(2)]
    rs = [[None] * 7 for _ in range(2)]
    near = {1: xp, -1: xm}
    way = (1, -1)

    def assemble(r):
        sib[r].wait_recv()
        theirs = sib_x[r].astype(F32)
        left = jnp.where(c == 0, mine[r], theirs)
        right = jnp.where(c == 0, theirs, mine[r])
        wide = jnp.concatenate([left, right], axis=1)
        xg[r, chip] = wide.astype(BF16)

    def gather(r, number, part, target):
        part = xg.at[r, part]
        ag[r][number] = send(AG + 7 * r + number, part, part, target)

    assemble(0)
    gather(0, 0, chip, core(xp, zh))
    gather(0, 1, chip, core(xm, zh))
    gather(0, 2, chip, core(x, zo))
    assemble(1)
    gather(1, 1, chip, core(xm, zh))
    gather(1, 2, chip, core(x, zo))

    def square(r, j, first=False):
        squares = xg[r, j].astype(F32)
        squares = squares * squares
        parts = squares[:, 0:128]
        for k in range(1, 5):
            parts = parts + squares[:, k * 128 : (k + 1) * 128]
        ss[r] = parts if first else ss[r] + parts

    def project(r, xs, zs):
        columns = pl.ds(pl.multiple_of(block(xs, zs) * WIDE, WIDE), WIDE)
        return jnp.dot(ctx[r], wo[:, columns], preferred_element_type=F32)

    def attend(r):
        total = jnp.sum(ss[r], axis=1, keepdims=True)
        inverse = lax.rsqrt(total * (1.0 / D) + EPS)
        for j in range(CHIPS):
            at = slice(j * WIDE, (j + 1) * WIDE)
            xn[:, at] = (xg[r, j].astype(F32) * inverse * gains[0:1, at]).astype(BF16)
        ours, theirs = qb_mine[...].astype(F32)[None, :], qb_theirs[...].astype(F32)[None, :]
        for p in range(2):
            bias = jnp.where(c == p, ours, theirs)
            q_ref[p] = (
                jnp.dot(xn[...], wq[p], preferred_element_type=F32) + bias
            ).astype(BF16)
        ours, theirs = vb_mine[...].astype(F32)[None, :], vb_theirs[...].astype(F32)[None, :]
        v_bias = jnp.concatenate(
            [jnp.where(c == 0, ours, theirs), jnp.where(c == 0, theirs, ours)], axis=1
        )
        key_value = dot_nt(xn[...], wkv[...])
        k_ref[0:ROWS, :] = key_value[:, 0:HS].astype(BF16)
        v_ref[0:ROWS, :] = (key_value[:, HS:] + v_bias).astype(BF16)
        length = lengths[2 * c + r]
        valid = lax.broadcasted_iota(jnp.int32, (ROWS, LANES), 1) < length
        for n in range(4):
            at = slice((n % 2) * HS, (n % 2 + 1) * HS)
            scores = dot_nt(q_ref[n // 2, :, at], k_ref[...]) * HS ** (-0.5)
            scores = jnp.where(valid, scores, F32(-1e30))
            peak = jnp.max(scores, axis=1, keepdims=True)
            expo = jnp.exp(scores - peak)
            prob = (expo / jnp.sum(expo, axis=1, keepdims=True)).astype(BF16)
            ctx[r, :, n * HS : (n + 1) * HS] = jnp.dot(
                prob, v_ref[...], preferred_element_type=F32
            ).astype(BF16)

    def put(r, slot, value, target):
        stage[r, slot] = value.astype(BF16)
        rs[r][slot] = send(RS + 7 * r + slot, stage.at[r, slot], got.at[r, slot], target)

    def take(r, slot):
        rs[r][slot].wait_recv()
        return got[r, slot].astype(F32)

    def first_sends(r):
        w = way[r]
        put(r, 0, project(r, xx, zo), core(x, zo))
        put(r, 1, project(r, xp, zo), core(xp, zh))
        put(r, 2, project(r, xm, zo), core(xm, zh))
        put(r, 3, project(r, near[-w], zh), core(near[-w], zh))

    def keep(r):
        kept[r, 0] = project(r, xx, zh)
        kept[r, 1] = project(r, x, zo)
        kept[r, 2] = project(r, near[way[r]], zh)
        kept[r, 3] = project(r, x, zh)

    square(0, chip, True)
    square(1, chip, True)
    ag[0][0].wait_recv()
    gather(0, 3, block(xm, zh), core(xp, zh))
    ag[0][2].wait_recv()
    gather(0, 4, block(x, zo), core(xp, zh))
    gather(0, 5, block(x, zo), core(xm, zh))
    gather(1, 0, chip, core(xp, zh))
    square(0, block(xm, zh))
    square(0, block(x, zo))
    ag[0][1].wait_recv()
    square(0, block(xp, zh))
    ag[1][1].wait_recv()
    gather(1, 3, block(xp, zh), core(xm, zh))
    ag[0][3].wait_recv()
    gather(0, 6, block(xx, zh), core(x, zo))
    ag[1][2].wait_recv()
    gather(1, 4, block(x, zo), core(xp, zh))
    gather(1, 5, block(x, zo), core(xm, zh))
    square(0, block(xx, zh))
    square(1, block(xp, zh))
    square(1, block(x, zo))
    for copy in local + later:
        copy.wait()
    for copy in sib_w:
        copy.wait_recv()
    gains[0:1, :] = attn_gain[...].astype(F32)[None, :]
    gains[1:2, :] = head_gain[...].astype(F32)[None, :]
    ag[0][5].wait_recv()
    square(0, block(xp, zo))
    ag[0][4].wait_recv()
    square(0, block(xm, zo))
    ag[0][6].wait_recv()
    square(0, block(xx, zo))
    attend(0)
    first_sends(0)
    ag[1][3].wait_recv()
    gather(1, 6, block(xx, zh), core(x, zo))
    head = [
        send(
            HEAD + d,
            wh_in.at[:, pl.ds(pl.multiple_of(other * WIDE, WIDE), WIDE)],
            whp.at[c, chip],
            {"tp": other * 2 + c},
        )
        for d, other in enumerate(others)
    ]
    keep(0)
    square(1, block(xx, zh))
    ag[1][0].wait_recv()
    square(1, block(xm, zh))
    ag[1][5].wait_recv()
    square(1, block(xp, zo))
    ag[1][4].wait_recv()
    square(1, block(xm, zo))
    ag[1][6].wait_recv()
    square(1, block(xx, zo))
    attend(1)
    first_sends(1)
    put(0, 4, kept[0, 0] + take(0, 0), core(near[way[0]], zh))
    keep(1)
    put(0, 5, kept[0, 1] + take(0, 1) + take(0, 2), core(x, zo))
    put(1, 4, kept[1, 0] + take(1, 0), core(near[way[1]], zh))
    put(0, 6, kept[0, 2] + take(0, 4), core(near[way[0]], zh))
    put(1, 5, kept[1, 1] + take(1, 1) + take(1, 2), core(x, zo))
    for copy in head:
        copy.wait_recv()
    sib_head = send(SIB_HEAD, whp.at[c], whp.at[c], sibling)
    put(1, 6, kept[1, 2] + take(1, 4), core(near[way[1]], zh))
    sib_head.wait_recv()
    gain = gains[1:2, pl.ds(pl.multiple_of(chip * WIDE, WIDE), WIDE)]
    for p in range(2):
        raw = whp[p].reshape(CHIPS * 32, WIDE).astype(F32)
        whg[p] = (raw * gain).astype(BF16)

    sib_hid = []
    logit = [[], []]
    for r in range(2):
        summed = kept[r, 3] + take(r, 3) + take(r, 6) + take(r, 5)
        hidden = (xg[r, chip].astype(F32) + summed).astype(BF16)
        hid[0:ROWS, :] = hidden
        for p in range(2):
            part = dot_nt(whg[p], hid[...]).astype(BF16)
            for i in range(CHIPS):
                lmsg[r, i, p * 32 : (p + 1) * 32, :] = part[i * 32 : (i + 1) * 32]
        squares = jnp.broadcast_to(lane_sums(hid[...].astype(F32)), (16, LANES))
        high = squares.astype(BF16).astype(F32)
        rest = squares - high
        mid = rest.astype(BF16).astype(F32)
        low = rest - mid
        row = lax.broadcasted_iota(jnp.int32, (16, LANES), 0)
        triple = jnp.where(
            row == 0, high, jnp.where(row == 1, mid, jnp.where(row == 2, low, 0.0))
        ).astype(BF16)
        for i in range(CHIPS):
            lmsg[r, i, 64:80, :] = triple
        for d, other in enumerate(others):
            logit[r].append(
                send(
                    LOGIT + 7 * r + d,
                    lmsg.at[r, other],
                    lgot.at[r, chip],
                    {"tp": other * 2 + c},
                )
            )
        lgot[r, chip] = lmsg[r, chip]
        left, right = hidden[:, 0:HALF], hidden[:, HALF:]
        hid_send[r] = jnp.where(c == 0, right, left)
        sib_hid.append(send(SIB_HID + r, hid_send.at[r], hid_got.at[r], sibling))
        hid_mine[r] = jnp.where(c == 0, left, right)

    for r in range(2):
        sib_hid[r].wait_recv()
        ours, theirs = hid_mine[r].astype(F32), hid_got[r].astype(F32)
        hid_all[L * r : L * (r + 1), :] = jnp.where(c == 0, ours, theirs)[0:L]
        hid_all[L * (r + 2) : L * (r + 3), :] = jnp.where(c == 0, theirs, ours)[0:L]
    for k in range(7):
        width = min(128, TOKENS - 128 * k)
        hid_out[:, 128 * k : 128 * k + width] = hid_all[128 * k : 128 * k + width, :].T.astype(
            BF16
        )

    logits = [None, None]
    smsg[...] = jnp.zeros_like(smsg)
    for r in range(2):
        for copy in logit[r]:
            copy.wait_recv()
        total = lgot[r, 0].astype(F32)
        for i in range(1, CHIPS):
            total = total + lgot[r, i].astype(F32)
        squares = total[64:65] + total[65:66] + total[66:67]
        inverse = lax.rsqrt(squares * (1.0 / D) + EPS)
        logits[r] = total[0:64] * inverse
        top = jnp.max(logits[r], axis=0, keepdims=True)
        smsg[2 * r : 2 * r + 1, :] = top
        smsg[2 * r + 1 : 2 * r + 2, :] = jnp.sum(
            jnp.exp(logits[r] - top), axis=0, keepdims=True
        )
    stats = [
        send(STAT + d, smsg, sgot.at[chip], {"tp": other * 2 + c})
        for d, other in enumerate(others)
    ]
    sgot[chip] = smsg[...]
    for copy in stats:
        copy.wait_recv()
    for r in range(2):
        tops = [sgot[i, 2 * r : 2 * r + 1, :] for i in range(CHIPS)]
        top = tops[0]
        for other_top in tops[1:]:
            top = jnp.maximum(top, other_top)
        mass = jnp.zeros((1, LANES), F32)
        for i in range(CHIPS):
            mass = mass + sgot[i, 2 * r + 1 : 2 * r + 2, :] * jnp.exp(tops[i] - top)
        logprob = logits[r] - (top + jnp.log(mass))
        first, second = logprob[0:32], logprob[32:64]
        lp_all[2 * c + r] = jnp.where(c == 0, first, second)
        lp_send[r] = jnp.where(c == 0, second, first)
    send(SIB_LP, lp_send, lp_all.at[pl.ds(2 * c, 2)], sibling).wait_recv()
    lp_out[...] = jnp.concatenate([lp_all[n, :, 0:L] for n in range(4)], axis=1)
    for copy in started:
        copy.wait_send()


def on_device(
    embeds,
    remask,
    lengths,
    mask_vec,
    attn_gain,
    w_query,
    q_bias,
    w_key,
    w_value,
    v_bias,
    w_out,
    head_gain,
    w_head,
):
    vmem = pl.BlockSpec(memory_space=pltpu.VMEM)
    anywhere = pl.BlockSpec(memory_space=pl.ANY)
    hidden, logprob = pl.pallas_call(
        kernel,
        out_shape=(
            jax.ShapeDtypeStruct((HALF, TOKENS), BF16),
            jax.ShapeDtypeStruct((32, TOKENS), F32),
        ),
        in_specs=[pl.BlockSpec(memory_space=pltpu.SMEM)] + [anywhere] * 12,
        out_specs=(vmem, vmem),
        scratch_shapes=[
            pltpu.VMEM((HALF, TOKENS), BF16),
            pltpu.VMEM((TOKENS,), jnp.int32),
            pltpu.VMEM((HALF,), BF16),
            pltpu.VMEM((D,), BF16),
            pltpu.VMEM((D,), BF16),
            pltpu.VMEM((256,), BF16),
            pltpu.VMEM((256,), BF16),
            pltpu.VMEM((64,), BF16),
            pltpu.VMEM((64,), BF16),
            pltpu.VMEM((8, D), F32),
            pltpu.VMEM((TOKENS + 8, HALF), F32),
            pltpu.VMEM((2, ROWS, HALF), F32),
            pltpu.VMEM((2, ROWS, HALF), BF16),
            pltpu.VMEM((2, ROWS, HALF), BF16),
            pltpu.VMEM((2, CHIPS, ROWS, WIDE), BF16),
            pltpu.VMEM((2, D, 256), BF16),
            pltpu.VMEM((256, D), BF16),
            pltpu.VMEM((512, D), BF16),
            pltpu.VMEM((2, CHIPS, 32, WIDE), BF16),
            pltpu.VMEM((2, CHIPS * 32, WIDE), BF16),
            pltpu.VMEM((ROWS, D), BF16),
            pltpu.VMEM((2, ROWS, 128), F32),
            pltpu.VMEM((2, ROWS, 256), BF16),
            pltpu.VMEM((LANES, HS), BF16),
            pltpu.VMEM((LANES, HS), BF16),
            pltpu.VMEM((2, ROWS, 512), BF16),
            pltpu.VMEM((2, 4, ROWS, WIDE), F32),
            pltpu.VMEM((2, 7, ROWS, WIDE), BF16),
            pltpu.VMEM((2, 7, ROWS, WIDE), BF16),
            pltpu.VMEM((LANES, WIDE), BF16),
            pltpu.VMEM((2, ROWS, HALF), BF16),
            pltpu.VMEM((2, ROWS, HALF), BF16),
            pltpu.VMEM((2, ROWS, HALF), BF16),
            pltpu.VMEM((TOKENS, HALF), F32),
            pltpu.VMEM((2, CHIPS, 80, LANES), BF16),
            pltpu.VMEM((2, CHIPS, 80, LANES), BF16),
            pltpu.VMEM((8, LANES), F32),
            pltpu.VMEM((CHIPS, 8, LANES), F32),
            pltpu.VMEM((2, 32, LANES), F32),
            pltpu.VMEM((4, 32, LANES), F32),
            pltpu.SemaphoreType.DMA((COPIES,)),
            pltpu.SemaphoreType.DMA((COPIES,)),
            pltpu.SemaphoreType.DMA((12,)),
        ],
        compiler_params=pltpu.CompilerParams(
            collective_id=0, has_side_effects=True, vmem_limit_bytes=56 << 20
        ),
        name="refine",
    )(
        lengths,
        embeds.T,
        remask,
        mask_vec,
        attn_gain,
        head_gain,
        q_bias,
        v_bias,
        w_query,
        w_key.T,
        w_value.T,
        w_out,
        w_head.T,
    )
    return hidden.T, logprob.T


def solution(mesh):
    placed = (
        P("rep", "tp"),
        P("rep"),
        P("rep"),
        P("tp"),
        P(),
        P(None, "tp"),
        P("tp"),
        P(None, "tp"),
        P(None, "tp"),
        P("tp"),
        P("tp", None),
        P(),
        P(None, "tp"),
    )
    return jax.shard_map(
        on_device,
        mesh=mesh,
        in_specs=placed,
        out_specs=(P("rep", "tp"), P("rep", "tp")),
        check_vma=False,
    )
```

```python
import jax
import jax.numpy as jnp
from jax import lax
from jax.experimental import pallas as pl
from jax.experimental.pallas import tpu as pltpu
from jax.sharding import PartitionSpec as P

HS = 128
L = 196
ROWS = 200
LANES = 256
CHIPS = 8
WIDE = 640
D = 5120
HALF = 320
TOKENS = 784
EPS = 1e-06
MESH = pl.DeviceIdType.MESH
F32 = jnp.float32
BF16 = jnp.bfloat16

SIB_X, SIB_WQ, SIB_WK, SIB_WV, SIB_WO, SIB_HEAD, SIB_QB, SIB_VB = 0, 2, 3, 4, 5, 6, 7, 8
AG = 9
RS = AG + 14
HEAD = RS + 14
LOGIT = HEAD + 7
STAT = LOGIT + 14
SIB_HID = STAT + 7
SIB_LP = SIB_HID + 2
COPIES = SIB_LP + 1


def dot_nt(a, b):
    return lax.dot_general(a, b, (((1,), (1,)), ((), ())), preferred_element_type=F32)


def lane_sums(wide):
    squares = wide * wide
    parts = squares[:, 0:128]
    for k in range(1, 5):
        parts = parts + squares[:, k * 128 : (k + 1) * 128]
    return jnp.sum(parts.T, axis=0, keepdims=True)


def kernel(
    lengths,
    embeds_in,
    remask_in,
    mask_vec_in,
    attn_gain_in,
    head_gain_in,
    qb_in,
    vb_in,
    wq_in,
    wk_in,
    wv_in,
    wo_in,
    wh_in,
    hid_out,
    lp_out,
    embeds,
    remask,
    mask_vec,
    attn_gain,
    head_gain,
    qb_mine,
    qb_theirs,
    vb_mine,
    vb_theirs,
    gains,
    masked,
    mine,
    sib_send,
    sib_x,
    xg,
    wq,
    wkv,
    wo,
    whp,
    whg,
    xn,
    ss,
    q_ref,
    k_ref,
    v_ref,
    ctx,
    kept,
    stage,
    got,
    hid,
    hid_send,
    hid_got,
    hid_mine,
    hid_all,
    lmsg,
    lgot,
    smsg,
    sgot,
    lp_send,
    lp_all,
    ssem,
    rsem,
    lsem,
):
    me = lax.axis_index("tp")
    x = me // 4
    zh = lax.rem(me // 2, 2)
    c = lax.rem(me, 2)
    chip = me // 2
    zo = 1 - zh
    xp, xm, xx = lax.rem(x + 1, 4), lax.rem(x + 3, 4), lax.rem(x + 2, 4)

    def core(xs, zs):
        return {"tp": xs * 4 + zs * 2 + c}

    def block(xs, zs):
        return xs * 2 + zs

    sibling = {"tp": me + 1 - 2 * c}
    others = [lax.rem(chip + d, CHIPS) for d in range(1, CHIPS)]
    started = []

    def send(number, src, dst, target):
        copy = pltpu.make_async_remote_copy(
            src_ref=src,
            dst_ref=dst,
            send_sem=ssem.at[number],
            recv_sem=rsem.at[number],
            device_id=target,
            device_id_type=MESH,
        )
        copy.start()
        started.append(copy)
        return copy

    barrier = pltpu.get_barrier_semaphore()
    pl.semaphore_signal(barrier, inc=1, device_id=sibling, device_id_type=MESH)
    for other in others:
        pl.semaphore_signal(
            barrier, inc=1, device_id={"tp": other * 2 + c}, device_id_type=MESH
        )
    krows = pl.ds(pl.multiple_of(c * 64, 64), 64)
    vrows = pl.ds(pl.multiple_of(128 + c * 64, 64), 64)
    orows = pl.ds(pl.multiple_of(c * 256, 256), 256)
    early = [
        pltpu.make_async_copy(embeds_in, embeds, lsem.at[0]),
        pltpu.make_async_copy(remask_in, remask, lsem.at[1]),
        pltpu.make_async_copy(mask_vec_in, mask_vec, lsem.at[2]),
    ]
    local = [
        pltpu.make_async_copy(attn_gain_in, attn_gain, lsem.at[3]),
        pltpu.make_async_copy(head_gain_in, head_gain, lsem.at[4]),
        pltpu.make_async_copy(qb_in, qb_mine, lsem.at[5]),
        pltpu.make_async_copy(vb_in, vb_mine, lsem.at[6]),
        pltpu.make_async_copy(wq_in, wq.at[c], lsem.at[7]),
        pltpu.make_async_copy(wk_in, wkv.at[krows], lsem.at[8]),
        pltpu.make_async_copy(wv_in, wkv.at[vrows], lsem.at[9]),
    ]
    later = [
        pltpu.make_async_copy(wo_in, wo.at[orows], lsem.at[10]),
        pltpu.make_async_copy(
            wh_in.at[:, pl.ds(pl.multiple_of(chip * WIDE, WIDE), WIDE)],
            whp.at[c, chip],
            lsem.at[11],
        ),
    ]
    for copy in early:
        copy.start()
    k_ref[ROWS:, :] = jnp.zeros((LANES - ROWS, HS), BF16)
    v_ref[ROWS:, :] = jnp.zeros((LANES - ROWS, HS), BF16)
    hid[ROWS:, :] = jnp.zeros((LANES - ROWS, WIDE), BF16)
    for copy in early:
        copy.wait()
    for copy in local + later:
        copy.start()
    flags = remask[...][None, :]
    fill = jnp.broadcast_to(mask_vec[...].astype(F32)[None, :], (8, HALF)).T[:, 0:1]
    masked[TOKENS:, :] = jnp.zeros((8, HALF), F32)
    for k in range(7):
        at = slice(128 * k, min(128 * (k + 1), TOKENS))
        masked[at, :] = jnp.where(flags[:, at] == 1, fill, embeds[:, at].astype(F32)).T
    for r in range(2):
        low, high = masked[L * r : L * r + ROWS], masked[L * (r + 2) : L * (r + 2) + ROWS]
        sib_send[r] = jnp.where(c == 0, high, low).astype(BF16)
    pl.semaphore_wait(barrier, CHIPS)

    sib = [send(SIB_X + r, sib_send.at[r], sib_x.at[r], sibling) for r in range(2)]
    head = [
        send(
            HEAD + d,
            wh_in.at[:, pl.ds(pl.multiple_of(other * WIDE, WIDE), WIDE)],
            whp.at[c, chip],
            {"tp": other * 2 + c},
        )
        for d, other in enumerate(others)
    ]
    sib_w = [
        send(SIB_QB, qb_in, qb_theirs, sibling),
        send(SIB_VB, vb_in, vb_theirs, sibling),
        send(SIB_WQ, wq_in, wq.at[c], sibling),
        send(SIB_WK, wk_in, wkv.at[krows], sibling),
        send(SIB_WV, wv_in, wkv.at[vrows], sibling),
        send(SIB_WO, wo_in, wo.at[orows], sibling),
    ]

    ag = [[None] * 7 for _ in range(2)]
    rs = [[None] * 7 for _ in range(2)]
    near = {1: xp, -1: xm}
    way = (1, -1)

    for r in range(2):
        low, high = masked[L * r : L * r + ROWS], masked[L * (r + 2) : L * (r + 2) + ROWS]
        mine[r] = jnp.where(c == 0, low, high)

    def assemble(r):
        sib[r].wait_recv()
        theirs = sib_x[r].astype(F32)
        left = jnp.where(c == 0, mine[r], theirs)
        right = jnp.where(c == 0, theirs, mine[r])
        wide = jnp.concatenate([left, right], axis=1)
        xg[r, chip] = wide.astype(BF16)

    def gather(r, number, part, target):
        part = xg.at[r, part]
        ag[r][number] = send(AG + 7 * r + number, part, part, target)

    assemble(0)
    gather(0, 0, chip, core(xp, zh))
    gather(0, 1, chip, core(xm, zh))
    gather(0, 2, chip, core(x, zo))
    assemble(1)
    gather(1, 1, chip, core(xm, zh))
    gather(1, 2, chip, core(x, zo))

    def square(r, j, first=False):
        squares = xg[r, j].astype(F32)
        squares = squares * squares
        parts = squares[:, 0:128]
        for k in range(1, 5):
            parts = parts + squares[:, k * 128 : (k + 1) * 128]
        ss[r] = parts if first else ss[r] + parts

    def project(r, xs, zs):
        columns = pl.ds(pl.multiple_of(block(xs, zs) * WIDE, WIDE), WIDE)
        return jnp.dot(ctx[r], wo[:, columns], preferred_element_type=F32)

    def attend(r):
        total = jnp.sum(ss[r], axis=1, keepdims=True)
        inverse = lax.rsqrt(total * (1.0 / D) + EPS)
        for j in range(CHIPS):
            at = slice(j * WIDE, (j + 1) * WIDE)
            xn[:, at] = (xg[r, j].astype(F32) * inverse * gains[0:1, at]).astype(BF16)
        ours, theirs = qb_mine[...].astype(F32)[None, :], qb_theirs[...].astype(F32)[None, :]
        for p in range(2):
            bias = jnp.where(c == p, ours, theirs)
            q_ref[p] = (
                jnp.dot(xn[...], wq[p], preferred_element_type=F32) + bias
            ).astype(BF16)
        ours, theirs = vb_mine[...].astype(F32)[None, :], vb_theirs[...].astype(F32)[None, :]
        v_bias = jnp.concatenate(
            [jnp.where(c == 0, ours, theirs), jnp.where(c == 0, theirs, ours)], axis=1
        )
        key_value = dot_nt(xn[...], wkv[...])
        k_ref[0:ROWS, :] = key_value[:, 0:HS].astype(BF16)
        v_ref[0:ROWS, :] = (key_value[:, HS:] + v_bias).astype(BF16)
        length = lengths[2 * c + r]
        valid = lax.broadcasted_iota(jnp.int32, (ROWS, LANES), 1) < length
        for n in range(4):
            at = slice((n % 2) * HS, (n % 2 + 1) * HS)
            scores = dot_nt(q_ref[n // 2, :, at], k_ref[...]) * HS ** (-0.5)
            scores = jnp.where(valid, scores, F32(-1e30))
            peak = jnp.max(scores, axis=1, keepdims=True)
            expo = jnp.exp(scores - peak)
            prob = (expo / jnp.sum(expo, axis=1, keepdims=True)).astype(BF16)
            ctx[r, :, n * HS : (n + 1) * HS] = jnp.dot(
                prob, v_ref[...], preferred_element_type=F32
            ).astype(BF16)

    def put(r, slot, value, target):
        stage[r, slot] = value.astype(BF16)
        rs[r][slot] = send(RS + 7 * r + slot, stage.at[r, slot], got.at[r, slot], target)

    def take(r, slot):
        rs[r][slot].wait_recv()
        return got[r, slot].astype(F32)

    def first_sends(r):
        w = way[r]
        put(r, 0, project(r, xx, zo), core(x, zo))
        put(r, 1, project(r, xp, zo), core(xp, zh))
        put(r, 2, project(r, xm, zo), core(xm, zh))
        put(r, 3, project(r, near[-w], zh), core(near[-w], zh))

    def keep(r):
        kept[r, 0] = project(r, xx, zh)
        kept[r, 1] = project(r, x, zo)
        kept[r, 2] = project(r, near[way[r]], zh)
        kept[r, 3] = project(r, x, zh)

    square(0, chip, True)
    square(1, chip, True)
    ag[0][0].wait_recv()
    gather(0, 3, block(xm, zh), core(xp, zh))
    ag[0][2].wait_recv()
    gather(0, 4, block(x, zo), core(xp, zh))
    gather(0, 5, block(x, zo), core(xm, zh))
    gather(1, 0, chip, core(xp, zh))
    square(0, block(xm, zh))
    square(0, block(x, zo))
    ag[0][1].wait_recv()
    square(0, block(xp, zh))
    ag[1][1].wait_recv()
    gather(1, 3, block(xp, zh), core(xm, zh))
    ag[0][3].wait_recv()
    gather(0, 6, block(xx, zh), core(x, zo))
    ag[1][2].wait_recv()
    gather(1, 4, block(x, zo), core(xp, zh))
    gather(1, 5, block(x, zo), core(xm, zh))
    square(0, block(xx, zh))
    square(1, block(xp, zh))
    square(1, block(x, zo))
    for copy in local + later:
        copy.wait()
    for copy in sib_w:
        copy.wait_recv()
    gains[0:1, :] = attn_gain[...].astype(F32)[None, :]
    gains[1:2, :] = head_gain[...].astype(F32)[None, :]
    for copy in head:
        copy.wait_recv()
    sib_head = send(SIB_HEAD, whp.at[c], whp.at[c], sibling)
    ag[0][5].wait_recv()
    square(0, block(xp, zo))
    ag[0][4].wait_recv()
    square(0, block(xm, zo))
    ag[0][6].wait_recv()
    square(0, block(xx, zo))
    attend(0)
    first_sends(0)
    ag[1][3].wait_recv()
    gather(1, 6, block(xx, zh), core(x, zo))
    keep(0)
    sib_head.wait_recv()
    gain = gains[1:2, pl.ds(pl.multiple_of(chip * WIDE, WIDE), WIDE)]
    for p in range(2):
        raw = whp[p].reshape(CHIPS * 32, WIDE).astype(F32)
        whg[p] = (raw * gain).astype(BF16)

    square(1, block(xx, zh))
    ag[1][0].wait_recv()
    square(1, block(xm, zh))
    ag[1][5].wait_recv()
    square(1, block(xp, zo))
    ag[1][4].wait_recv()
    square(1, block(xm, zo))
    ag[1][6].wait_recv()
    square(1, block(xx, zo))
    put(0, 4, kept[0, 0] + take(0, 0), core(near[way[0]], zh))
    attend(1)
    first_sends(1)
    keep(1)
    put(0, 5, kept[0, 1] + take(0, 1) + take(0, 2), core(x, zo))
    put(1, 4, kept[1, 0] + take(1, 0), core(near[way[1]], zh))
    put(0, 6, kept[0, 2] + take(0, 4), core(near[way[0]], zh))
    put(1, 5, kept[1, 1] + take(1, 1) + take(1, 2), core(x, zo))
    put(1, 6, kept[1, 2] + take(1, 4), core(near[way[1]], zh))
    sib_hid = []
    logit = [[], []]
    for r in range(2):
        summed = kept[r, 3] + take(r, 3) + take(r, 6) + take(r, 5)
        hidden = (xg[r, chip].astype(F32) + summed).astype(BF16)
        hid[0:ROWS, :] = hidden
        for p in range(2):
            part = dot_nt(whg[p], hid[...]).astype(BF16)
            for i in range(CHIPS):
                lmsg[r, i, p * 32 : (p + 1) * 32, :] = part[i * 32 : (i + 1) * 32]
        squares = jnp.broadcast_to(lane_sums(hid[...].astype(F32)), (16, LANES))
        high = squares.astype(BF16).astype(F32)
        rest = squares - high
        mid = rest.astype(BF16).astype(F32)
        low = rest - mid
        row = lax.broadcasted_iota(jnp.int32, (16, LANES), 0)
        triple = jnp.where(
            row == 0, high, jnp.where(row == 1, mid, jnp.where(row == 2, low, 0.0))
        ).astype(BF16)
        for i in range(CHIPS):
            lmsg[r, i, 64:80, :] = triple
        for d, other in enumerate(others):
            logit[r].append(
                send(
                    LOGIT + 7 * r + d,
                    lmsg.at[r, other],
                    lgot.at[r, chip],
                    {"tp": other * 2 + c},
                )
            )
        lgot[r, chip] = lmsg[r, chip]
        left, right = hidden[:, 0:HALF], hidden[:, HALF:]
        hid_send[r] = jnp.where(c == 0, right, left)
        sib_hid.append(send(SIB_HID + r, hid_send.at[r], hid_got.at[r], sibling))
        hid_mine[r] = jnp.where(c == 0, left, right)

    for r in range(2):
        sib_hid[r].wait_recv()
        ours, theirs = hid_mine[r].astype(F32), hid_got[r].astype(F32)
        hid_all[L * r : L * (r + 1), :] = jnp.where(c == 0, ours, theirs)[0:L]
        hid_all[L * (r + 2) : L * (r + 3), :] = jnp.where(c == 0, theirs, ours)[0:L]
    for k in range(7):
        width = min(128, TOKENS - 128 * k)
        hid_out[:, 128 * k : 128 * k + width] = hid_all[128 * k : 128 * k + width, :].T.astype(
            BF16
        )

    logits = [None, None]
    smsg[...] = jnp.zeros_like(smsg)
    for r in range(2):
        for copy in logit[r]:
            copy.wait_recv()
        total = lgot[r, 0].astype(F32)
        for i in range(1, CHIPS):
            total = total + lgot[r, i].astype(F32)
        squares = total[64:65] + total[65:66] + total[66:67]
        inverse = lax.rsqrt(squares * (1.0 / D) + EPS)
        logits[r] = total[0:64] * inverse
        top = jnp.max(logits[r], axis=0, keepdims=True)
        smsg[2 * r : 2 * r + 1, :] = top
        smsg[2 * r + 1 : 2 * r + 2, :] = jnp.sum(
            jnp.exp(logits[r] - top), axis=0, keepdims=True
        )
    stats = [
        send(STAT + d, smsg, sgot.at[chip], {"tp": other * 2 + c})
        for d, other in enumerate(others)
    ]
    sgot[chip] = smsg[...]
    for copy in stats:
        copy.wait_recv()
    for r in range(2):
        tops = [sgot[i, 2 * r : 2 * r + 1, :] for i in range(CHIPS)]
        top = tops[0]
        for other_top in tops[1:]:
            top = jnp.maximum(top, other_top)
        mass = jnp.zeros((1, LANES), F32)
        for i in range(CHIPS):
            mass = mass + sgot[i, 2 * r + 1 : 2 * r + 2, :] * jnp.exp(tops[i] - top)
        logprob = logits[r] - (top + jnp.log(mass))
        first, second = logprob[0:32], logprob[32:64]
        lp_all[2 * c + r] = jnp.where(c == 0, first, second)
        lp_send[r] = jnp.where(c == 0, second, first)
    send(SIB_LP, lp_send, lp_all.at[pl.ds(2 * c, 2)], sibling).wait_recv()
    lp_out[...] = jnp.concatenate([lp_all[n, :, 0:L] for n in range(4)], axis=1)
    for copy in started:
        copy.wait_send()


def on_device(
    embeds,
    remask,
    lengths,
    mask_vec,
    attn_gain,
    w_query,
    q_bias,
    w_key,
    w_value,
    v_bias,
    w_out,
    head_gain,
    w_head,
):
    vmem = pl.BlockSpec(memory_space=pltpu.VMEM)
    anywhere = pl.BlockSpec(memory_space=pl.ANY)
    hidden, logprob = pl.pallas_call(
        kernel,
        out_shape=(
            jax.ShapeDtypeStruct((HALF, TOKENS), BF16),
            jax.ShapeDtypeStruct((32, TOKENS), F32),
        ),
        in_specs=[pl.BlockSpec(memory_space=pltpu.SMEM)] + [anywhere] * 12,
        out_specs=(vmem, vmem),
        scratch_shapes=[
            pltpu.VMEM((HALF, TOKENS), BF16),
            pltpu.VMEM((TOKENS,), jnp.int32),
            pltpu.VMEM((HALF,), BF16),
            pltpu.VMEM((D,), BF16),
            pltpu.VMEM((D,), BF16),
            pltpu.VMEM((256,), BF16),
            pltpu.VMEM((256,), BF16),
            pltpu.VMEM((64,), BF16),
            pltpu.VMEM((64,), BF16),
            pltpu.VMEM((8, D), F32),
            pltpu.VMEM((TOKENS + 8, HALF), F32),
            pltpu.VMEM((2, ROWS, HALF), F32),
            pltpu.VMEM((2, ROWS, HALF), BF16),
            pltpu.VMEM((2, ROWS, HALF), BF16),
            pltpu.VMEM((2, CHIPS, ROWS, WIDE), BF16),
            pltpu.VMEM((2, D, 256), BF16),
            pltpu.VMEM((256, D), BF16),
            pltpu.VMEM((512, D), BF16),
            pltpu.VMEM((2, CHIPS, 32, WIDE), BF16),
            pltpu.VMEM((2, CHIPS * 32, WIDE), BF16),
            pltpu.VMEM((ROWS, D), BF16),
            pltpu.VMEM((2, ROWS, 128), F32),
            pltpu.VMEM((2, ROWS, 256), BF16),
            pltpu.VMEM((LANES, HS), BF16),
            pltpu.VMEM((LANES, HS), BF16),
            pltpu.VMEM((2, ROWS, 512), BF16),
            pltpu.VMEM((2, 4, ROWS, WIDE), F32),
            pltpu.VMEM((2, 7, ROWS, WIDE), BF16),
            pltpu.VMEM((2, 7, ROWS, WIDE), BF16),
            pltpu.VMEM((LANES, WIDE), BF16),
            pltpu.VMEM((2, ROWS, HALF), BF16),
            pltpu.VMEM((2, ROWS, HALF), BF16),
            pltpu.VMEM((2, ROWS, HALF), BF16),
            pltpu.VMEM((TOKENS, HALF), F32),
            pltpu.VMEM((2, CHIPS, 80, LANES), BF16),
            pltpu.VMEM((2, CHIPS, 80, LANES), BF16),
            pltpu.VMEM((8, LANES), F32),
            pltpu.VMEM((CHIPS, 8, LANES), F32),
            pltpu.VMEM((2, 32, LANES), F32),
            pltpu.VMEM((4, 32, LANES), F32),
            pltpu.SemaphoreType.DMA((COPIES,)),
            pltpu.SemaphoreType.DMA((COPIES,)),
            pltpu.SemaphoreType.DMA((12,)),
        ],
        compiler_params=pltpu.CompilerParams(
            collective_id=0, has_side_effects=True, vmem_limit_bytes=56 << 20
        ),
        name="refine",
    )(
        lengths,
        embeds.T,
        remask,
        mask_vec,
        attn_gain,
        head_gain,
        q_bias,
        v_bias,
        w_query,
        w_key.T,
        w_value.T,
        w_out,
        w_head.T,
    )
    return hidden.T, logprob.T


def solution(mesh):
    placed = (
        P("rep", "tp"),
        P("rep"),
        P("rep"),
        P("tp"),
        P(),
        P(None, "tp"),
        P("tp"),
        P(None, "tp"),
        P(None, "tp"),
        P("tp"),
        P("tp", None),
        P(),
        P(None, "tp"),
    )
    return jax.shard_map(
        on_device,
        mesh=mesh,
        in_specs=placed,
        out_specs=(P("rep", "tp"), P("rep", "tp")),
        check_vma=False,
    )
```

```python
import jax
import jax.numpy as jnp
from jax import lax
from jax.experimental import pallas as pl
from jax.experimental.pallas import tpu as pltpu
from jax.sharding import PartitionSpec as P

HS = 128
L = 196
ROWS = 200
LANES = 256
CHIPS = 8
WIDE = 640
D = 5120
HALF = 320
TOKENS = 784
EPS = 1e-06
MESH = pl.DeviceIdType.MESH
F32 = jnp.float32
BF16 = jnp.bfloat16

SIB_X, SIB_WQ, SIB_WK, SIB_WV, SIB_WO, SIB_HEAD, SIB_QB, SIB_VB = 0, 2, 3, 4, 5, 6, 7, 8
AG = 9
RS = AG + 14
HEAD = RS + 14
LOGIT = HEAD + 7
STAT = LOGIT + 14
SIB_HID = STAT + 15
SIB_LP = SIB_HID + 2
PARTS = SIB_LP + 1
COPIES = PARTS + 12
PART_ROWS = (slice(0, 96), slice(96, ROWS))


def dot_nt(a, b):
    return lax.dot_general(a, b, (((1,), (1,)), ((), ())), preferred_element_type=F32)


def lane_sums(wide):
    squares = wide * wide
    parts = squares[:, 0:128]
    for k in range(1, 5):
        parts = parts + squares[:, k * 128 : (k + 1) * 128]
    return jnp.sum(parts.T, axis=0, keepdims=True)


def kernel(
    lengths,
    embeds_in,
    remask_in,
    mask_vec_in,
    attn_gain_in,
    head_gain_in,
    qb_in,
    vb_in,
    wq_in,
    wk_in,
    wv_in,
    wo_in,
    wh_in,
    hid_out,
    lp_out,
    embeds,
    remask,
    mask_vec,
    attn_gain,
    head_gain,
    qb_mine,
    qb_theirs,
    vb_mine,
    vb_theirs,
    gains,
    masked,
    mine,
    sib_send,
    sib_x,
    xg,
    wq,
    wkv,
    wo,
    whp,
    whg,
    xn,
    ss,
    q_ref,
    k_ref,
    v_ref,
    ctx,
    kept,
    stage,
    got,
    hid,
    hid_send,
    hid_got,
    hid_mine,
    hid_all,
    lmsg,
    lgot,
    smsg,
    sgot,
    lp_send,
    lp_got,
    ssem,
    rsem,
    lsem,
):
    me = lax.axis_index("tp")
    x = me // 4
    zh = lax.rem(me // 2, 2)
    c = lax.rem(me, 2)
    chip = me // 2
    zo = 1 - zh
    xp, xm, xx = lax.rem(x + 1, 4), lax.rem(x + 3, 4), lax.rem(x + 2, 4)

    def core(xs, zs):
        return {"tp": xs * 4 + zs * 2 + c}

    def block(xs, zs):
        return xs * 2 + zs

    sibling = {"tp": me + 1 - 2 * c}
    others = [lax.rem(chip + d, CHIPS) for d in range(1, CHIPS)]
    started = []

    def send(number, src, dst, target):
        copy = pltpu.make_async_remote_copy(
            src_ref=src,
            dst_ref=dst,
            send_sem=ssem.at[number],
            recv_sem=rsem.at[number],
            device_id=target,
            device_id_type=MESH,
        )
        copy.start()
        started.append(copy)
        return copy

    barrier = pltpu.get_barrier_semaphore()
    pl.semaphore_signal(barrier, inc=1, device_id=sibling, device_id_type=MESH)
    for nd in (core(xp, zh), core(xm, zh), core(x, zo)):
        pl.semaphore_signal(barrier, inc=1, device_id=nd, device_id_type=MESH)
    krows = pl.ds(pl.multiple_of(c * 64, 64), 64)
    vrows = pl.ds(pl.multiple_of(128 + c * 64, 64), 64)
    orows = pl.ds(pl.multiple_of(c * 256, 256), 256)
    early = [
        pltpu.make_async_copy(embeds_in, embeds, lsem.at[0]),
        pltpu.make_async_copy(remask_in, remask, lsem.at[1]),
        pltpu.make_async_copy(mask_vec_in, mask_vec, lsem.at[2]),
    ]
    local = [
        pltpu.make_async_copy(attn_gain_in, attn_gain, lsem.at[3]),
        pltpu.make_async_copy(head_gain_in, head_gain, lsem.at[4]),
        pltpu.make_async_copy(qb_in, qb_mine, lsem.at[5]),
        pltpu.make_async_copy(vb_in, vb_mine, lsem.at[6]),
        pltpu.make_async_copy(wq_in, wq.at[c], lsem.at[7]),
        pltpu.make_async_copy(wk_in, wkv.at[krows], lsem.at[8]),
        pltpu.make_async_copy(wv_in, wkv.at[vrows], lsem.at[9]),
    ]
    later = [
        pltpu.make_async_copy(wo_in, wo.at[orows], lsem.at[10]),
        pltpu.make_async_copy(
            wh_in.at[:, pl.ds(pl.multiple_of(chip * WIDE, WIDE), WIDE)],
            whp.at[c, chip],
            lsem.at[11],
        ),
    ]
    for copy in early:
        copy.start()
    k_ref[ROWS:, :] = jnp.zeros((LANES - ROWS, HS), BF16)
    v_ref[ROWS:, :] = jnp.zeros((LANES - ROWS, HS), BF16)
    hid[ROWS:, :] = jnp.zeros((LANES - ROWS, WIDE), BF16)
    for copy in early:
        copy.wait()
    for copy in local + later:
        copy.start()
    flags = remask[...][None, :]
    fill = jnp.broadcast_to(mask_vec[...].astype(F32)[None, :], (8, HALF)).T[:, 0:1]
    masked[TOKENS:, :] = jnp.zeros((8, HALF), F32)

    def prepare(tiles, r):
        for k in tiles:
            at = slice(128 * k, min(128 * (k + 1), TOKENS))
            tile = jnp.where(flags[:, at] == 1, fill, embeds[:, at].astype(F32))
            masked[at, :] = tile.T
        low, high = masked[L * r : L * r + ROWS], masked[L * (r + 2) : L * (r + 2) + ROWS]
        sib_send[r] = jnp.where(c == 0, high, low).astype(BF16)

    def pick(r):
        low, high = masked[L * r : L * r + ROWS], masked[L * (r + 2) : L * (r + 2) + ROWS]
        mine[r] = jnp.where(c == 0, low, high)

    prepare((0, 1, 3, 4), 0)
    pl.semaphore_wait(barrier, 4)

    sib = [send(SIB_X, sib_send.at[0], sib_x.at[0], sibling)]
    pick(0)
    prepare((2, 5, 6), 1)
    sib.append(send(SIB_X + 1, sib_send.at[1], sib_x.at[1], sibling))
    sib_w = [
        send(SIB_QB, qb_in, qb_theirs, sibling),
        send(SIB_VB, vb_in, vb_theirs, sibling),
        send(SIB_WQ, wq_in, wq.at[c], sibling),
        send(SIB_WK, wk_in, wkv.at[krows], sibling),
        send(SIB_WV, wv_in, wkv.at[vrows], sibling),
        send(SIB_WO, wo_in, wo.at[orows], sibling),
    ]

    ag = [[None] * 7 for _ in range(2)]
    rs = [[None] * 7 for _ in range(2)]
    rs_part = {}
    near = {1: xp, -1: xm}
    way = (1, -1)

    def assemble(r):
        sib[r].wait_recv()
        theirs = sib_x[r].astype(F32)
        left = jnp.where(c == 0, mine[r], theirs)
        right = jnp.where(c == 0, theirs, mine[r])
        wide = jnp.concatenate([left, right], axis=1)
        xg[r, chip] = wide.astype(BF16)

    def gather(r, number, part, target):
        part = xg.at[r, part]
        ag[r][number] = send(AG + 7 * r + number, part, part, target)

    assemble(0)
    gather(0, 0, chip, core(xp, zh))
    gather(0, 1, chip, core(xm, zh))
    gather(0, 2, chip, core(x, zo))
    pick(1)
    assemble(1)
    gather(1, 1, chip, core(xm, zh))
    gather(1, 2, chip, core(x, zo))

    def square(r, j, first=False):
        squares = xg[r, j].astype(F32)
        squares = squares * squares
        parts = squares[:, 0:128]
        for k in range(1, 5):
            parts = parts + squares[:, k * 128 : (k + 1) * 128]
        ss[r] = parts if first else ss[r] + parts

    def project(r, xs, zs):
        columns = pl.ds(pl.multiple_of(block(xs, zs) * WIDE, WIDE), WIDE)
        return jnp.dot(ctx[r], wo[:, columns], preferred_element_type=F32)

    def attend(r):
        total = jnp.sum(ss[r], axis=1, keepdims=True)
        inverse = lax.rsqrt(total * (1.0 / D) + EPS)
        for j in range(CHIPS):
            at = slice(j * WIDE, (j + 1) * WIDE)
            xn[:, at] = (xg[r, j].astype(F32) * inverse * gains[0:1, at]).astype(BF16)
        ours, theirs = qb_mine[...].astype(F32)[None, :], qb_theirs[...].astype(F32)[None, :]
        for p in range(2):
            bias = jnp.where(c == p, ours, theirs)
            q_ref[p] = (
                jnp.dot(xn[...], wq[p], preferred_element_type=F32) + bias
            ).astype(BF16)
        ours, theirs = vb_mine[...].astype(F32)[None, :], vb_theirs[...].astype(F32)[None, :]
        v_bias = jnp.concatenate(
            [jnp.where(c == 0, ours, theirs), jnp.where(c == 0, theirs, ours)], axis=1
        )
        key_value = dot_nt(xn[...], wkv[...])
        k_ref[0:ROWS, :] = key_value[:, 0:HS].astype(BF16)
        v_ref[0:ROWS, :] = (key_value[:, HS:] + v_bias).astype(BF16)
        length = lengths[2 * c + r]
        valid = lax.broadcasted_iota(jnp.int32, (ROWS, LANES), 1) < length
        for n in range(4):
            at = slice((n % 2) * HS, (n % 2 + 1) * HS)
            scores = dot_nt(q_ref[n // 2, :, at], k_ref[...]) * HS ** (-0.5)
            scores = jnp.where(valid, scores, F32(-1e30))
            peak = jnp.max(scores, axis=1, keepdims=True)
            expo = jnp.exp(scores - peak)
            prob = (expo / jnp.sum(expo, axis=1, keepdims=True)).astype(BF16)
            ctx[r, :, n * HS : (n + 1) * HS] = jnp.dot(
                prob, v_ref[...], preferred_element_type=F32
            ).astype(BF16)

    def put(r, slot, value, target):
        stage[r, slot] = value.astype(BF16)
        rs[r][slot] = send(RS + 7 * r + slot, stage.at[r, slot], got.at[r, slot], target)

    def put_part(r, slot, n, value, target):
        at = PART_ROWS[n]
        stage[r, slot, at] = value.astype(BF16)
        number = PARTS + 6 * r + (0, 0, 0, 0, 2, 0, 4)[slot] + n
        src, dst = stage.at[r, slot, at], got.at[r, slot, at]
        rs_part[r, slot, n] = send(number, src, dst, target)

    def relay(r, slot, own, source, target):
        for n, at in enumerate(PART_ROWS):
            rs_part[r, source, n].wait_recv()
            value = kept[r, own, at] + got[r, source, at].astype(F32)
            put_part(r, slot, n, value, target)

    def take(r, slot):
        if slot == 6:
            for n in range(2):
                rs_part[r, slot, n].wait_recv()
        else:
            rs[r][slot].wait_recv()
        return got[r, slot].astype(F32)

    def first_sends(r):
        w = way[r]
        value = project(r, xx, zo)
        for n, at in enumerate(PART_ROWS):
            put_part(r, 0, n, value[at], core(x, zo))
        put(r, 1, project(r, xp, zo), core(xp, zh))
        put(r, 2, project(r, xm, zo), core(xm, zh))
        if r == 0:
            put(r, 3, project(r, near[-w], zh), core(near[-w], zh))

    def keep(r):
        kept[r, 0] = project(r, xx, zh)
        kept[r, 1] = project(r, x, zo)
        kept[r, 2] = project(r, near[way[r]], zh)
        kept[r, 3] = project(r, x, zh)

    square(0, chip, True)
    square(1, chip, True)
    ag[0][0].wait_recv()
    gather(0, 3, block(xm, zh), core(xp, zh))
    ag[0][2].wait_recv()
    gather(0, 4, block(x, zo), core(xp, zh))
    gather(0, 5, block(x, zo), core(xm, zh))
    gather(1, 0, chip, core(xp, zh))
    square(0, block(xm, zh))
    square(0, block(x, zo))
    ag[0][1].wait_recv()
    square(0, block(xp, zh))
    ag[1][1].wait_recv()
    gather(1, 3, block(xp, zh), core(xm, zh))
    ag[0][3].wait_recv()
    gather(0, 6, block(xx, zh), core(x, zo))
    ag[1][2].wait_recv()
    gather(1, 4, block(x, zo), core(xp, zh))
    gather(1, 5, block(x, zo), core(xm, zh))
    square(0, block(xx, zh))
    square(1, block(xp, zh))
    square(1, block(x, zo))
    for copy in local + later:
        copy.wait()
    for copy in sib_w:
        copy.wait_recv()
    gains[0:1, :] = attn_gain[...].astype(F32)[None, :]
    gains[1:2, :] = head_gain[...].astype(F32)[None, :]
    ag[0][5].wait_recv()
    square(0, block(xp, zo))
    ag[0][4].wait_recv()
    square(0, block(xm, zo))
    ag[0][6].wait_recv()
    square(0, block(xx, zo))
    attend(0)
    first_sends(0)
    ag[1][3].wait_recv()
    gather(1, 6, block(xx, zh), core(x, zo))
    head = [
        send(
            HEAD + d,
            wh_in.at[:, pl.ds(pl.multiple_of(other * WIDE, WIDE), WIDE)],
            whp.at[c, chip],
            {"tp": other * 2 + c},
        )
        for d, other in enumerate(others)
    ]
    keep(0)
    square(1, block(xx, zh))
    ag[1][0].wait_recv()
    square(1, block(xm, zh))
    ag[1][5].wait_recv()
    square(1, block(xp, zo))
    ag[1][4].wait_recv()
    square(1, block(xm, zo))
    ag[1][6].wait_recv()
    square(1, block(xx, zo))
    relay(0, 4, 0, 0, core(near[way[0]], zh))
    attend(1)
    first_sends(1)
    keep(1)
    put(0, 5, kept[0, 1] + take(0, 1) + take(0, 2), core(x, zo))
    relay(1, 4, 0, 0, core(near[way[1]], zh))
    relay(0, 6, 2, 4, core(near[way[0]], zh))
    put(1, 3, project(1, near[-way[1]], zh), core(near[-way[1]], zh))
    put(1, 5, kept[1, 1] + take(1, 1) + take(1, 2), core(x, zo))
    for copy in head:
        copy.wait_recv()
    sib_head = send(SIB_HEAD, whp.at[c], whp.at[c], sibling)
    relay(1, 6, 2, 4, core(near[way[1]], zh))
    sib_head.wait_recv()
    gain = gains[1:2, pl.ds(pl.multiple_of(chip * WIDE, WIDE), WIDE)]
    for p in range(2):
        raw = whp[p].reshape(CHIPS * 32, WIDE).astype(F32)
        whg[p] = (raw * gain).astype(BF16)

    sib_hid = []
    logit = [[], []]
    for r in range(2):
        summed = kept[r, 3] + take(r, 3) + take(r, 6) + take(r, 5)
        hidden = (xg[r, chip].astype(F32) + summed).astype(BF16)
        hid[0:ROWS, :] = hidden
        for p in range(2):
            part = dot_nt(whg[p], hid[...]).astype(BF16)
            for i in range(CHIPS):
                lmsg[r, i, p * 32 : (p + 1) * 32, :] = part[i * 32 : (i + 1) * 32]
        squares = jnp.broadcast_to(lane_sums(hid[...].astype(F32)), (16, LANES))
        high = squares.astype(BF16).astype(F32)
        rest = squares - high
        mid = rest.astype(BF16).astype(F32)
        low = rest - mid
        row = lax.broadcasted_iota(jnp.int32, (16, LANES), 0)
        triple = jnp.where(
            row == 0, high, jnp.where(row == 1, mid, jnp.where(row == 2, low, 0.0))
        ).astype(BF16)
        for i in range(CHIPS):
            lmsg[r, i, 64:80, :] = triple
        for d, other in enumerate(others):
            logit[r].append(
                send(
                    LOGIT + 7 * r + d,
                    lmsg.at[r, other],
                    lgot.at[r, chip],
                    {"tp": other * 2 + c},
                )
            )
        lgot[r, chip] = lmsg[r, chip]
        left, right = hidden[:, 0:HALF], hidden[:, HALF:]
        hid_send[r] = jnp.where(c == 0, right, left)
        sib_hid.append(send(SIB_HID + r, hid_send.at[r], hid_got.at[r], sibling))
        hid_mine[r] = jnp.where(c == 0, left, right)

    for r in range(2):
        sib_hid[r].wait_recv()
        ours, theirs = hid_mine[r].astype(F32), hid_got[r].astype(F32)
        hid_all[L * r : L * (r + 1), :] = jnp.where(c == 0, ours, theirs)[0:L]
        hid_all[L * (r + 2) : L * (r + 3), :] = jnp.where(c == 0, theirs, ours)[0:L]
    for k in range(7):
        width = min(128, TOKENS - 128 * k)
        hid_out[:, 128 * k : 128 * k + width] = hid_all[128 * k : 128 * k + width, :].T.astype(
            BF16
        )

    logits = [None, None]
    smsg[...] = jnp.zeros_like(smsg)
    for r in range(2):
        for copy in logit[r]:
            copy.wait_recv()
        total = lgot[r, 0].astype(F32)
        for i in range(1, CHIPS):
            total = total + lgot[r, i].astype(F32)
        squares = total[64:65] + total[65:66] + total[66:67]
        inverse = lax.rsqrt(squares * (1.0 / D) + EPS)
        logits[r] = total[0:64] * inverse
        top = jnp.max(logits[r], axis=0, keepdims=True)
        smsg[2 * r : 2 * r + 1, :] = top
        smsg[2 * r + 1 : 2 * r + 2, :] = jnp.sum(
            jnp.exp(logits[r] - top), axis=0, keepdims=True
        )
    stats = []
    for d, other in enumerate(others):
        for k in range(2):
            target = {"tp": other * 2 + (c if k == 0 else 1 - c)}
            stats.append(send(STAT + 2 * d + k, smsg, sgot.at[c, chip], target))
    stats.append(send(STAT + 14, smsg, sgot.at[c, chip], sibling))
    sgot[c, chip] = smsg[...]
    for r in range(2):
        lp_send[r] = jnp.where(c == 0, logits[r][32:64], logits[r][0:32])
    sib_lp = send(SIB_LP, lp_send, lp_got, sibling)
    for copy in stats:
        copy.wait_recv()
    sib_lp.wait_recv()
    pieces = []
    for n in range(4):
        plane, r = n // 2, n % 2
        tops = [sgot[plane, i, 2 * r : 2 * r + 1, :] for i in range(CHIPS)]
        top = tops[0]
        for other_top in tops[1:]:
            top = jnp.maximum(top, other_top)
        mass = jnp.zeros((1, LANES), F32)
        for i in range(CHIPS):
            share = sgot[plane, i, 2 * r + 1 : 2 * r + 2, :]
            mass = mass + share * jnp.exp(tops[i] - top)
        ours = jnp.where(c == 0, logits[r][0:32], logits[r][32:64])
        piece = jnp.where(c == plane, ours, lp_got[r]) - (top + jnp.log(mass))
        pieces.append(piece[:, 0:L])
    lp_out[...] = jnp.concatenate(pieces, axis=1)
    for copy in started:
        copy.wait_send()


def on_device(
    embeds,
    remask,
    lengths,
    mask_vec,
    attn_gain,
    w_query,
    q_bias,
    w_key,
    w_value,
    v_bias,
    w_out,
    head_gain,
    w_head,
):
    vmem = pl.BlockSpec(memory_space=pltpu.VMEM)
    anywhere = pl.BlockSpec(memory_space=pl.ANY)
    hidden, logprob = pl.pallas_call(
        kernel,
        out_shape=(
            jax.ShapeDtypeStruct((HALF, TOKENS), BF16),
            jax.ShapeDtypeStruct((32, TOKENS), F32),
        ),
        in_specs=[pl.BlockSpec(memory_space=pltpu.SMEM)] + [anywhere] * 12,
        out_specs=(vmem, vmem),
        scratch_shapes=[
            pltpu.VMEM((HALF, TOKENS), BF16),
            pltpu.VMEM((TOKENS,), jnp.int32),
            pltpu.VMEM((HALF,), BF16),
            pltpu.VMEM((D,), BF16),
            pltpu.VMEM((D,), BF16),
            pltpu.VMEM((256,), BF16),
            pltpu.VMEM((256,), BF16),
            pltpu.VMEM((64,), BF16),
            pltpu.VMEM((64,), BF16),
            pltpu.VMEM((8, D), F32),
            pltpu.VMEM((TOKENS + 8, HALF), F32),
            pltpu.VMEM((2, ROWS, HALF), F32),
            pltpu.VMEM((2, ROWS, HALF), BF16),
            pltpu.VMEM((2, ROWS, HALF), BF16),
            pltpu.VMEM((2, CHIPS, ROWS, WIDE), BF16),
            pltpu.VMEM((2, D, 256), BF16),
            pltpu.VMEM((256, D), BF16),
            pltpu.VMEM((512, D), BF16),
            pltpu.VMEM((2, CHIPS, 32, WIDE), BF16),
            pltpu.VMEM((2, CHIPS * 32, WIDE), BF16),
            pltpu.VMEM((ROWS, D), BF16),
            pltpu.VMEM((2, ROWS, 128), F32),
            pltpu.VMEM((2, ROWS, 256), BF16),
            pltpu.VMEM((LANES, HS), BF16),
            pltpu.VMEM((LANES, HS), BF16),
            pltpu.VMEM((2, ROWS, 512), BF16),
            pltpu.VMEM((2, 4, ROWS, WIDE), F32),
            pltpu.VMEM((2, 7, ROWS, WIDE), BF16),
            pltpu.VMEM((2, 7, ROWS, WIDE), BF16),
            pltpu.VMEM((LANES, WIDE), BF16),
            pltpu.VMEM((2, ROWS, HALF), BF16),
            pltpu.VMEM((2, ROWS, HALF), BF16),
            pltpu.VMEM((2, ROWS, HALF), BF16),
            pltpu.VMEM((TOKENS, HALF), F32),
            pltpu.VMEM((2, CHIPS, 80, LANES), BF16),
            pltpu.VMEM((2, CHIPS, 80, LANES), BF16),
            pltpu.VMEM((8, LANES), F32),
            pltpu.VMEM((2, CHIPS, 8, LANES), F32),
            pltpu.VMEM((2, 32, LANES), F32),
            pltpu.VMEM((2, 32, LANES), F32),
            pltpu.SemaphoreType.DMA((COPIES,)),
            pltpu.SemaphoreType.DMA((COPIES,)),
            pltpu.SemaphoreType.DMA((12,)),
        ],
        compiler_params=pltpu.CompilerParams(
            collective_id=0, has_side_effects=True, vmem_limit_bytes=56 << 20
        ),
        name="refine",
    )(
        lengths,
        embeds.T,
        remask,
        mask_vec,
        attn_gain,
        head_gain,
        q_bias,
        v_bias,
        w_query,
        w_key.T,
        w_value.T,
        w_out,
        w_head.T,
    )
    return hidden.T, logprob.T


def solution(mesh):
    placed = (
        P("rep", "tp"),
        P("rep"),
        P("rep"),
        P("tp"),
        P(),
        P(None, "tp"),
        P("tp"),
        P(None, "tp"),
        P(None, "tp"),
        P("tp"),
        P("tp", None),
        P(),
        P(None, "tp"),
    )
    return jax.shard_map(
        on_device,
        mesh=mesh,
        in_specs=placed,
        out_specs=(P("rep", "tp"), P("rep", "tp")),
        check_vma=False,
    )
```

```python
import jax
import jax.numpy as jnp
from jax import lax
from jax.experimental import pallas as pl
from jax.experimental.pallas import tpu as pltpu
from jax.sharding import PartitionSpec as P

HS = 128
L = 196
ROWS = 200
LANES = 256
CHIPS = 8
WIDE = 640
D = 5120
HALF = 320
TOKENS = 784
EPS = 1e-06
MESH = pl.DeviceIdType.MESH
F32 = jnp.float32
BF16 = jnp.bfloat16

SIB_X, SIB_WQ, SIB_WK, SIB_WV, SIB_WO, SIB_HEAD, SIB_QB, SIB_VB = 0, 2, 3, 4, 5, 6, 7, 8
AG = 9
RS = AG + 14
HEAD = RS + 14
LOGIT = HEAD + 7
STAT = LOGIT + 14
SIB_HID = STAT + 15
SIB_LP = SIB_HID + 2
PARTS = SIB_LP + 1
COPIES = PARTS + 12
PART_ROWS = (slice(0, 96), slice(96, ROWS))


def dot_nt(a, b):
    return lax.dot_general(a, b, (((1,), (1,)), ((), ())), preferred_element_type=F32)


def lane_sums(wide):
    squares = wide * wide
    parts = squares[:, 0:128]
    for k in range(1, 5):
        parts = parts + squares[:, k * 128 : (k + 1) * 128]
    return jnp.sum(parts.T, axis=0, keepdims=True)


def kernel(
    lengths,
    embeds_in,
    remask_in,
    mask_vec_in,
    attn_gain_in,
    head_gain_in,
    qb_in,
    vb_in,
    wq_in,
    wk_in,
    wv_in,
    wo_in,
    wh_in,
    hid_out,
    lp_out,
    embeds,
    remask,
    mask_vec,
    attn_gain,
    head_gain,
    qb_mine,
    qb_theirs,
    vb_mine,
    vb_theirs,
    gains,
    masked,
    mine,
    sib_send,
    sib_x,
    xg,
    wq,
    wkv,
    wo,
    whp,
    whg,
    xn,
    ss,
    q_ref,
    k_ref,
    v_ref,
    ctx,
    kept,
    stage,
    got,
    hid,
    hid_send,
    hid_got,
    hid_mine,
    hid_all,
    lmsg,
    lgot,
    smsg,
    sgot,
    lp_send,
    lp_got,
    ssem,
    rsem,
    lsem,
):
    me = lax.axis_index("tp")
    x = me // 4
    zh = lax.rem(me // 2, 2)
    c = lax.rem(me, 2)
    chip = me // 2
    zo = 1 - zh
    xp, xm, xx = lax.rem(x + 1, 4), lax.rem(x + 3, 4), lax.rem(x + 2, 4)

    def core(xs, zs):
        return {"tp": xs * 4 + zs * 2 + c}

    def block(xs, zs):
        return xs * 2 + zs

    sibling = {"tp": me + 1 - 2 * c}
    others = [lax.rem(chip + d, CHIPS) for d in (5, 3, 4, 1, 7, 2, 6)]
    started = []

    def send(number, src, dst, target):
        copy = pltpu.make_async_remote_copy(
            src_ref=src,
            dst_ref=dst,
            send_sem=ssem.at[number],
            recv_sem=rsem.at[number],
            device_id=target,
            device_id_type=MESH,
        )
        copy.start()
        started.append(copy)
        return copy

    barrier = pltpu.get_barrier_semaphore()
    pl.semaphore_signal(barrier, inc=1, device_id=sibling, device_id_type=MESH)
    for nd in (core(xp, zh), core(xm, zh), core(x, zo)):
        pl.semaphore_signal(barrier, inc=1, device_id=nd, device_id_type=MESH)
    krows = pl.ds(pl.multiple_of(c * 64, 64), 64)
    vrows = pl.ds(pl.multiple_of(128 + c * 64, 64), 64)
    orows = pl.ds(pl.multiple_of(c * 256, 256), 256)
    early = [
        pltpu.make_async_copy(embeds_in, embeds, lsem.at[0]),
        pltpu.make_async_copy(remask_in, remask, lsem.at[1]),
        pltpu.make_async_copy(mask_vec_in, mask_vec, lsem.at[2]),
    ]
    local = [
        pltpu.make_async_copy(attn_gain_in, attn_gain, lsem.at[3]),
        pltpu.make_async_copy(head_gain_in, head_gain, lsem.at[4]),
        pltpu.make_async_copy(qb_in, qb_mine, lsem.at[5]),
        pltpu.make_async_copy(vb_in, vb_mine, lsem.at[6]),
        pltpu.make_async_copy(wq_in, wq.at[c], lsem.at[7]),
        pltpu.make_async_copy(wk_in, wkv.at[krows], lsem.at[8]),
        pltpu.make_async_copy(wv_in, wkv.at[vrows], lsem.at[9]),
    ]
    later = [
        pltpu.make_async_copy(wo_in, wo.at[orows], lsem.at[10]),
        pltpu.make_async_copy(
            wh_in.at[:, pl.ds(pl.multiple_of(chip * WIDE, WIDE), WIDE)],
            whp.at[c, chip],
            lsem.at[11],
        ),
    ]
    for copy in early:
        copy.start()
    k_ref[ROWS:, :] = jnp.zeros((LANES - ROWS, HS), BF16)
    v_ref[ROWS:, :] = jnp.zeros((LANES - ROWS, HS), BF16)
    hid[ROWS:, :] = jnp.zeros((LANES - ROWS, WIDE), BF16)
    for copy in early:
        copy.wait()
    for copy in local + later:
        copy.start()
    flags = remask[...][None, :]
    fill = jnp.broadcast_to(mask_vec[...].astype(F32)[None, :], (8, HALF)).T[:, 0:1]
    masked[TOKENS:, :] = jnp.zeros((8, HALF), F32)

    def prepare(tiles, r):
        for k in tiles:
            at = slice(128 * k, min(128 * (k + 1), TOKENS))
            tile = jnp.where(flags[:, at] == 1, fill, embeds[:, at].astype(F32))
            masked[at, :] = tile.T
        low, high = masked[L * r : L * r + ROWS], masked[L * (r + 2) : L * (r + 2) + ROWS]
        sib_send[r] = jnp.where(c == 0, high, low).astype(BF16)

    def pick(r):
        low, high = masked[L * r : L * r + ROWS], masked[L * (r + 2) : L * (r + 2) + ROWS]
        mine[r] = jnp.where(c == 0, low, high)

    prepare((0, 1, 3, 4), 0)
    pl.semaphore_wait(barrier, 4)

    sib = [send(SIB_X, sib_send.at[0], sib_x.at[0], sibling)]
    pick(0)
    prepare((2, 5, 6), 1)
    sib.append(send(SIB_X + 1, sib_send.at[1], sib_x.at[1], sibling))
    sib_w = [
        send(SIB_QB, qb_in, qb_theirs, sibling),
        send(SIB_VB, vb_in, vb_theirs, sibling),
        send(SIB_WQ, wq_in, wq.at[c], sibling),
        send(SIB_WK, wk_in, wkv.at[krows], sibling),
        send(SIB_WV, wv_in, wkv.at[vrows], sibling),
        send(SIB_WO, wo_in, wo.at[orows], sibling),
    ]

    ag = [[None] * 7 for _ in range(2)]
    rs = [[None] * 7 for _ in range(2)]
    rs_part = {}
    near = {1: xp, -1: xm}
    way = (1, -1)

    def assemble(r):
        sib[r].wait_recv()
        theirs = sib_x[r].astype(F32)
        left = jnp.where(c == 0, mine[r], theirs)
        right = jnp.where(c == 0, theirs, mine[r])
        wide = jnp.concatenate([left, right], axis=1)
        xg[r, chip] = wide.astype(BF16)

    def gather(r, number, part, target):
        part = xg.at[r, part]
        ag[r][number] = send(AG + 7 * r + number, part, part, target)

    assemble(0)
    gather(0, 0, chip, core(xp, zh))
    gather(0, 1, chip, core(xm, zh))
    gather(0, 2, chip, core(x, zo))
    pick(1)
    assemble(1)
    gather(1, 1, chip, core(xm, zh))
    gather(1, 2, chip, core(x, zo))

    def square(r, j, first=False):
        squares = xg[r, j].astype(F32)
        squares = squares * squares
        parts = squares[:, 0:128]
        for k in range(1, 5):
            parts = parts + squares[:, k * 128 : (k + 1) * 128]
        ss[r] = parts if first else ss[r] + parts

    def project(r, xs, zs):
        columns = pl.ds(pl.multiple_of(block(xs, zs) * WIDE, WIDE), WIDE)
        return jnp.dot(ctx[r], wo[:, columns], preferred_element_type=F32)

    def attend(r):
        total = jnp.sum(ss[r], axis=1, keepdims=True)
        inverse = lax.rsqrt(total * (1.0 / D) + EPS)
        for j in range(CHIPS):
            at = slice(j * WIDE, (j + 1) * WIDE)
            xn[:, at] = (xg[r, j].astype(F32) * inverse * gains[0:1, at]).astype(BF16)
        ours, theirs = qb_mine[...].astype(F32)[None, :], qb_theirs[...].astype(F32)[None, :]
        for p in range(2):
            bias = jnp.where(c == p, ours, theirs)
            q_ref[p] = (
                jnp.dot(xn[...], wq[p], preferred_element_type=F32) + bias
            ).astype(BF16)
        ours, theirs = vb_mine[...].astype(F32)[None, :], vb_theirs[...].astype(F32)[None, :]
        v_bias = jnp.concatenate(
            [jnp.where(c == 0, ours, theirs), jnp.where(c == 0, theirs, ours)], axis=1
        )
        key_value = dot_nt(xn[...], wkv[...])
        k_ref[0:ROWS, :] = key_value[:, 0:HS].astype(BF16)
        v_ref[0:ROWS, :] = (key_value[:, HS:] + v_bias).astype(BF16)
        length = lengths[2 * c + r]
        valid = lax.broadcasted_iota(jnp.int32, (ROWS, LANES), 1) < length
        for n in range(4):
            at = slice((n % 2) * HS, (n % 2 + 1) * HS)
            scores = dot_nt(q_ref[n // 2, :, at], k_ref[...]) * HS ** (-0.5)
            scores = jnp.where(valid, scores, F32(-1e30))
            peak = jnp.max(scores, axis=1, keepdims=True)
            expo = jnp.exp(scores - peak)
            prob = (expo / jnp.sum(expo, axis=1, keepdims=True)).astype(BF16)
            ctx[r, :, n * HS : (n + 1) * HS] = jnp.dot(
                prob, v_ref[...], preferred_element_type=F32
            ).astype(BF16)

    def put(r, slot, value, target):
        stage[r, slot] = value.astype(BF16)
        rs[r][slot] = send(RS + 7 * r + slot, stage.at[r, slot], got.at[r, slot], target)

    def put_part(r, slot, n, value, target):
        at = PART_ROWS[n]
        stage[r, slot, at] = value.astype(BF16)
        number = PARTS + 6 * r + (0, 0, 0, 0, 2, 0, 4)[slot] + n
        src, dst = stage.at[r, slot, at], got.at[r, slot, at]
        rs_part[r, slot, n] = send(number, src, dst, target)

    def relay(r, slot, own, source, target):
        for n, at in enumerate(PART_ROWS):
            rs_part[r, source, n].wait_recv()
            value = kept[r, own, at] + got[r, source, at].astype(F32)
            put_part(r, slot, n, value, target)

    def take(r, slot):
        if slot == 6:
            for n in range(2):
                rs_part[r, slot, n].wait_recv()
        else:
            rs[r][slot].wait_recv()
        return got[r, slot].astype(F32)

    def first_sends(r):
        w = way[r]
        value = project(r, xx, zo)
        for n, at in enumerate(PART_ROWS):
            put_part(r, 0, n, value[at], core(x, zo))
        put(r, 1, project(r, xp, zo), core(xp, zh))
        put(r, 2, project(r, xm, zo), core(xm, zh))
        if r == 0:
            put(r, 3, project(r, near[-w], zh), core(near[-w], zh))

    def keep(r):
        kept[r, 0] = project(r, xx, zh)
        kept[r, 1] = project(r, x, zo)
        kept[r, 2] = project(r, near[way[r]], zh)
        kept[r, 3] = project(r, x, zh)

    square(0, chip, True)
    square(1, chip, True)
    ag[0][0].wait_recv()
    gather(0, 3, block(xm, zh), core(xp, zh))
    ag[0][2].wait_recv()
    gather(0, 4, block(x, zo), core(xp, zh))
    gather(0, 5, block(x, zo), core(xm, zh))
    gather(1, 0, chip, core(xp, zh))
    square(0, block(xm, zh))
    square(0, block(x, zo))
    ag[0][1].wait_recv()
    square(0, block(xp, zh))
    ag[1][1].wait_recv()
    gather(1, 3, block(xp, zh), core(xm, zh))
    ag[0][3].wait_recv()
    gather(0, 6, block(xx, zh), core(x, zo))
    ag[1][2].wait_recv()
    gather(1, 4, block(x, zo), core(xp, zh))
    gather(1, 5, block(x, zo), core(xm, zh))
    square(0, block(xx, zh))
    square(1, block(xp, zh))
    square(1, block(x, zo))
    for copy in local + later:
        copy.wait()
    for copy in sib_w:
        copy.wait_recv()
    gains[0:1, :] = attn_gain[...].astype(F32)[None, :]
    gains[1:2, :] = head_gain[...].astype(F32)[None, :]
    ag[0][5].wait_recv()
    square(0, block(xp, zo))
    ag[0][4].wait_recv()
    square(0, block(xm, zo))
    ag[0][6].wait_recv()
    square(0, block(xx, zo))
    attend(0)
    first_sends(0)
    ag[1][3].wait_recv()
    gather(1, 6, block(xx, zh), core(x, zo))
    head = [
        send(
            HEAD + d,
            wh_in.at[:, pl.ds(pl.multiple_of(other * WIDE, WIDE), WIDE)],
            whp.at[c, chip],
            {"tp": other * 2 + c},
        )
        for d, other in enumerate(others)
    ]
    keep(0)
    square(1, block(xx, zh))
    ag[1][0].wait_recv()
    square(1, block(xm, zh))
    ag[1][5].wait_recv()
    square(1, block(xp, zo))
    ag[1][4].wait_recv()
    square(1, block(xm, zo))
    ag[1][6].wait_recv()
    square(1, block(xx, zo))
    relay(0, 4, 0, 0, core(near[way[0]], zh))
    attend(1)
    first_sends(1)
    keep(1)
    put(0, 5, kept[0, 1] + take(0, 1) + take(0, 2), core(x, zo))
    relay(1, 4, 0, 0, core(near[way[1]], zh))
    relay(0, 6, 2, 4, core(near[way[0]], zh))
    put(1, 3, project(1, near[-way[1]], zh), core(near[-way[1]], zh))
    put(1, 5, kept[1, 1] + take(1, 1) + take(1, 2), core(x, zo))
    for copy in head:
        copy.wait_recv()
    sib_head = send(SIB_HEAD, whp.at[c], whp.at[c], sibling)
    relay(1, 6, 2, 4, core(near[way[1]], zh))
    sib_head.wait_recv()
    gain = gains[1:2, pl.ds(pl.multiple_of(chip * WIDE, WIDE), WIDE)]
    for p in range(2):
        raw = whp[p].reshape(CHIPS * 32, WIDE).astype(F32)
        whg[p] = (raw * gain).astype(BF16)

    sib_hid = []
    logit = [[], []]
    for r in range(2):
        summed = kept[r, 3] + take(r, 3) + take(r, 6) + take(r, 5)
        hidden = (xg[r, chip].astype(F32) + summed).astype(BF16)
        hid[0:ROWS, :] = hidden
        for p in range(2):
            part = dot_nt(whg[p], hid[...]).astype(BF16)
            for i in range(CHIPS):
                lmsg[r, i, p * 32 : (p + 1) * 32, :] = part[i * 32 : (i + 1) * 32]
        squares = jnp.broadcast_to(lane_sums(hid[...].astype(F32)), (16, LANES))
        high = squares.astype(BF16).astype(F32)
        rest = squares - high
        mid = rest.astype(BF16).astype(F32)
        low = rest - mid
        row = lax.broadcasted_iota(jnp.int32, (16, LANES), 0)
        triple = jnp.where(
            row == 0, high, jnp.where(row == 1, mid, jnp.where(row == 2, low, 0.0))
        ).astype(BF16)
        for i in range(CHIPS):
            lmsg[r, i, 64:80, :] = triple
        for d, other in enumerate(others):
            logit[r].append(
                send(
                    LOGIT + 7 * r + d,
                    lmsg.at[r, other],
                    lgot.at[r, chip],
                    {"tp": other * 2 + c},
                )
            )
        lgot[r, chip] = lmsg[r, chip]
        left, right = hidden[:, 0:HALF], hidden[:, HALF:]
        hid_send[r] = jnp.where(c == 0, right, left)
        sib_hid.append(send(SIB_HID + r, hid_send.at[r], hid_got.at[r], sibling))
        hid_mine[r] = jnp.where(c == 0, left, right)

    for r in range(2):
        sib_hid[r].wait_recv()
        ours, theirs = hid_mine[r].astype(F32), hid_got[r].astype(F32)
        hid_all[L * r : L * (r + 1), :] = jnp.where(c == 0, ours, theirs)[0:L]
        hid_all[L * (r + 2) : L * (r + 3), :] = jnp.where(c == 0, theirs, ours)[0:L]
    for k in range(7):
        width = min(128, TOKENS - 128 * k)
        hid_out[:, 128 * k : 128 * k + width] = hid_all[128 * k : 128 * k + width, :].T.astype(
            BF16
        )

    logits = [None, None]
    smsg[...] = jnp.zeros_like(smsg)
    for r in range(2):
        for copy in logit[r]:
            copy.wait_recv()
        total = lgot[r, 0].astype(F32)
        for i in range(1, CHIPS):
            total = total + lgot[r, i].astype(F32)
        squares = total[64:65] + total[65:66] + total[66:67]
        inverse = lax.rsqrt(squares * (1.0 / D) + EPS)
        logits[r] = total[0:64] * inverse
        top = jnp.max(logits[r], axis=0, keepdims=True)
        smsg[2 * r : 2 * r + 1, :] = top
        smsg[2 * r + 1 : 2 * r + 2, :] = jnp.sum(
            jnp.exp(logits[r] - top), axis=0, keepdims=True
        )
    stats = []
    for d, other in enumerate(others):
        for k in range(2):
            target = {"tp": other * 2 + (c if k == 0 else 1 - c)}
            stats.append(send(STAT + 2 * d + k, smsg, sgot.at[c, chip], target))
    stats.append(send(STAT + 14, smsg, sgot.at[c, chip], sibling))
    sgot[c, chip] = smsg[...]
    for r in range(2):
        lp_send[r] = jnp.where(c == 0, logits[r][32:64], logits[r][0:32])
    sib_lp = send(SIB_LP, lp_send, lp_got, sibling)
    for copy in stats:
        copy.wait_recv()
    sib_lp.wait_recv()
    pieces = []
    for n in range(4):
        plane, r = n // 2, n % 2
        tops = [sgot[plane, i, 2 * r : 2 * r + 1, :] for i in range(CHIPS)]
        top = tops[0]
        for other_top in tops[1:]:
            top = jnp.maximum(top, other_top)
        mass = jnp.zeros((1, LANES), F32)
        for i in range(CHIPS):
            share = sgot[plane, i, 2 * r + 1 : 2 * r + 2, :]
            mass = mass + share * jnp.exp(tops[i] - top)
        ours = jnp.where(c == 0, logits[r][0:32], logits[r][32:64])
        piece = jnp.where(c == plane, ours, lp_got[r]) - (top + jnp.log(mass))
        pieces.append(piece[:, 0:L])
    lp_out[...] = jnp.concatenate(pieces, axis=1)
    for copy in started:
        copy.wait_send()


def on_device(
    embeds,
    remask,
    lengths,
    mask_vec,
    attn_gain,
    w_query,
    q_bias,
    w_key,
    w_value,
    v_bias,
    w_out,
    head_gain,
    w_head,
):
    vmem = pl.BlockSpec(memory_space=pltpu.VMEM)
    anywhere = pl.BlockSpec(memory_space=pl.ANY)
    hidden, logprob = pl.pallas_call(
        kernel,
        out_shape=(
            jax.ShapeDtypeStruct((HALF, TOKENS), BF16),
            jax.ShapeDtypeStruct((32, TOKENS), F32),
        ),
        in_specs=[pl.BlockSpec(memory_space=pltpu.SMEM)] + [anywhere] * 12,
        out_specs=(vmem, vmem),
        scratch_shapes=[
            pltpu.VMEM((HALF, TOKENS), BF16),
            pltpu.VMEM((TOKENS,), jnp.int32),
            pltpu.VMEM((HALF,), BF16),
            pltpu.VMEM((D,), BF16),
            pltpu.VMEM((D,), BF16),
            pltpu.VMEM((256,), BF16),
            pltpu.VMEM((256,), BF16),
            pltpu.VMEM((64,), BF16),
            pltpu.VMEM((64,), BF16),
            pltpu.VMEM((8, D), F32),
            pltpu.VMEM((TOKENS + 8, HALF), F32),
            pltpu.VMEM((2, ROWS, HALF), F32),
            pltpu.VMEM((2, ROWS, HALF), BF16),
            pltpu.VMEM((2, ROWS, HALF), BF16),
            pltpu.VMEM((2, CHIPS, ROWS, WIDE), BF16),
            pltpu.VMEM((2, D, 256), BF16),
            pltpu.VMEM((256, D), BF16),
            pltpu.VMEM((512, D), BF16),
            pltpu.VMEM((2, CHIPS, 32, WIDE), BF16),
            pltpu.VMEM((2, CHIPS * 32, WIDE), BF16),
            pltpu.VMEM((ROWS, D), BF16),
            pltpu.VMEM((2, ROWS, 128), F32),
            pltpu.VMEM((2, ROWS, 256), BF16),
            pltpu.VMEM((LANES, HS), BF16),
            pltpu.VMEM((LANES, HS), BF16),
            pltpu.VMEM((2, ROWS, 512), BF16),
            pltpu.VMEM((2, 4, ROWS, WIDE), F32),
            pltpu.VMEM((2, 7, ROWS, WIDE), BF16),
            pltpu.VMEM((2, 7, ROWS, WIDE), BF16),
            pltpu.VMEM((LANES, WIDE), BF16),
            pltpu.VMEM((2, ROWS, HALF), BF16),
            pltpu.VMEM((2, ROWS, HALF), BF16),
            pltpu.VMEM((2, ROWS, HALF), BF16),
            pltpu.VMEM((TOKENS, HALF), F32),
            pltpu.VMEM((2, CHIPS, 80, LANES), BF16),
            pltpu.VMEM((2, CHIPS, 80, LANES), BF16),
            pltpu.VMEM((8, LANES), F32),
            pltpu.VMEM((2, CHIPS, 8, LANES), F32),
            pltpu.VMEM((2, 32, LANES), F32),
            pltpu.VMEM((2, 32, LANES), F32),
            pltpu.SemaphoreType.DMA((COPIES,)),
            pltpu.SemaphoreType.DMA((COPIES,)),
            pltpu.SemaphoreType.DMA((12,)),
        ],
        compiler_params=pltpu.CompilerParams(
            collective_id=0, has_side_effects=True, vmem_limit_bytes=56 << 20
        ),
        name="refine",
    )(
        lengths,
        embeds.T,
        remask,
        mask_vec,
        attn_gain,
        head_gain,
        q_bias,
        v_bias,
        w_query,
        w_key.T,
        w_value.T,
        w_out,
        w_head.T,
    )
    return hidden.T, logprob.T


def solution(mesh):
    placed = (
        P("rep", "tp"),
        P("rep"),
        P("rep"),
        P("tp"),
        P(),
        P(None, "tp"),
        P("tp"),
        P(None, "tp"),
        P(None, "tp"),
        P("tp"),
        P("tp", None),
        P(),
        P(None, "tp"),
    )
    return jax.shard_map(
        on_device,
        mesh=mesh,
        in_specs=placed,
        out_specs=(P("rep", "tp"), P("rep", "tp")),
        check_vma=False,
    )
```
